256 devices in a mesh: sub: 8 (over y, z_lo), row: 16 (over x, z_hi), col: 2 (over core).
Axes of the slice: x: 4, y: 4, z: 8 (z_hi: 4, z_lo: 2; z = z_hi * 2 + z_lo), core: 2. Of those that a mesh axis runs over, the one named last changes fastest.
Arguments:
- child_pivot: float32 [8, 1024, 1024], P('sub', 'row'), as said below
- child_border: float32 [8, 4096, 1024], P('sub', 'row'), as said below
- child_update: float32 [8, 4096, 4096], P('sub', 'row', 'col'), as said below
- parent_front: float32 [16384, 16384], P('row', ('sub', 'col')), as said below
- tile_map: int32 [8, 32], replicated, may hold values from -1 to 127, as said below
Outputs:
- schur_block: float32 [16384, 16384], P('row', ('sub', 'col'))
- panel_rows: float32 [16384, 256], P('row')
The draws below stay inside these ranges and needn't reach their ends.
Inputs may be any that keep to these rules, and one draw needn't show every extreme that they name: For each child s the matrix [[child_pivot[s], child_border[s]^T], [child_border[s], child_update[s]]] is symmetric positive definite; child_pivot[s] and child_update[s] are symmetric. `child_border`: see child_pivot: the border of a symmetric positive definite child front. `child_update`: see child_pivot: the trailing block of a symmetric positive definite child front. `parent_front`: symmetric positive definite. tile_map[s, t] is the parent tile that receives tile t of child s, or -1 where t lies beyond child s's front; the -1 entries of a child come after its live ones, every child has 16 live tiles or more, some child has all 32 live and some exactly 16; the live entries of one child are distinct; the child tiles t with t // 2 == i map into parent tiles i * 8 to (i + 1) * 8 - 1.
All inputs are finite; a program needn't handle non-finite values.
Results may differ from the reference program's by a relative error of at most 0.0001.
Values sent between devices are 32-bit elements; how exact they have to be, the bound alone decides.
No kernel may reach another device: no remote copies, remote signals or barrier semaphores. Data moves between devices by JAX's collectives and lax.ppermute only.
A program may use at most 128 MiB of HBM per device.

```python
import math
import jax
import jax.numpy as jnp
from jax import lax

PIVOTS = 1024
CONTRIB = 4096
PARENT = 16384
PANEL = 256
TILE = 128
CHILDREN = 8
CTILES = 32
CT_ROW = 2
PT_ROW = 8


def entries(key, shape, sigma):
    values = jax.random.normal(key, shape, jnp.float32)
    return values * sigma


def child_sigma():
    return 1.5 / math.sqrt(PIVOTS + CONTRIB)


def symmetric_blocks(key, salt, count, sigma, low, high):
    raw = entries(jax.random.fold_in(key, salt), (CHILDREN, count, count), sigma)
    mirrored = (raw + jnp.swapaxes(raw, 1, 2)) * 0.70710678
    diagonal = jax.random.uniform(jax.random.fold_in(key, salt + 1), (CHILDREN, count), jnp.float32, low, high)
    unit = jnp.eye(count, dtype=jnp.float32)
    return mirrored * (1.0 - unit) + diagonal[:, :, None] * unit


def draw_child_pivot(key, part):
    block = symmetric_blocks(key, 21, PIVOTS, child_sigma(), 4.5, 6.0)
    return block


def draw_child_border(key, part):
    raw = entries(jax.random.fold_in(key, 23), (CHILDREN, CONTRIB, PIVOTS), child_sigma())
    return raw


def draw_child_update(key, part):
    block = symmetric_blocks(key, 25, CONTRIB, child_sigma(), 4.5, 6.0)
    return block


def draw_parent_front(key, part):
    raw = entries(jax.random.fold_in(key, 41), (PARENT, PARENT), 1.0 / math.sqrt(PARENT))
    mirrored = (raw + raw.T) * 0.70710678
    diagonal = jax.random.uniform(jax.random.fold_in(key, 42), (PARENT,), jnp.float32, 2.5, 3.5)
    unit = jnp.eye(PARENT, dtype=jnp.float32)
    block = mirrored * (1.0 - unit) + diagonal[:, None] * unit
    return block


def draw_tile_map(key, part):
    block_count = CTILES // CT_ROW
    total_blocks = CHILDREN * block_count
    perm_keys = jax.random.split(jax.random.fold_in(key, 5), total_blocks)
    ranked = jax.vmap(lambda subkey: jax.random.permutation(subkey, PT_ROW))(perm_keys)[:, :CT_ROW]
    lower_keys = jax.random.split(jax.random.fold_in(key, 8), total_blocks)
    lower_ranked = jax.vmap(lambda subkey: jax.random.permutation(subkey, PT_ROW - 1))(lower_keys)[:, :CT_ROW - 1]
    with_last = jnp.concatenate([lower_ranked.astype(jnp.int32), jnp.full((total_blocks, 1), PT_ROW - 1, jnp.int32)], axis=1)
    order_keys = jax.random.split(jax.random.fold_in(key, 9), total_blocks)
    orders = jax.vmap(lambda subkey: jax.random.permutation(subkey, CT_ROW))(order_keys).astype(jnp.int32)
    forced = jnp.take_along_axis(with_last, orders, axis=1)
    shuffle = jax.random.permutation(jax.random.fold_in(key, 7), CHILDREN)
    child_ids = jnp.arange(CHILDREN, dtype=jnp.int32)[:, None] * jnp.ones((1, block_count), jnp.int32)
    block_ids = jnp.ones((CHILDREN, 1), jnp.int32) * jnp.arange(block_count, dtype=jnp.int32)[None, :]
    target = ((child_ids == shuffle[0]) & (block_ids == block_count - 1)).reshape(total_blocks)
    picked = jnp.where(target[:, None], forced, ranked.astype(jnp.int32))
    block_start = jnp.arange(block_count, dtype=jnp.int32) * PT_ROW
    chosen = picked.reshape(CHILDREN, block_count, CT_ROW) + block_start[None, :, None]
    chosen = chosen.reshape(CHILDREN, CTILES)
    live_count = jax.random.randint(jax.random.fold_in(key, 6), (CHILDREN,), CTILES // 2, CTILES + 1)
    live_count = live_count.at[shuffle[0]].set(CTILES).at[shuffle[1]].set(CTILES // 2)
    positions = jnp.arange(CTILES, dtype=jnp.int32)
    return jnp.where(positions[None, :] < live_count[:, None], chosen, -1).astype(jnp.int32)


def setup_inputs(seed: int = 0) -> dict:
    splits = jax.random.split(jax.random.key(seed), 6)
    child_pivot = draw_child_pivot(jax.random.fold_in(splits[5], 71), 0)
    child_border = draw_child_border(jax.random.fold_in(splits[5], 71), 0)
    child_update = draw_child_update(jax.random.fold_in(splits[5], 71), 0)
    parent_front = draw_parent_front(jax.random.fold_in(splits[5], 71), 0)
    tile_map = draw_tile_map(jax.random.fold_in(splits[5], 71), 0)
    return dict(child_pivot=child_pivot, child_border=child_border, child_update=child_update, parent_front=parent_front, tile_map=tile_map)


highest = lax.Precision.HIGHEST

def solve_rows(lower_tri, right_rows):
    return jax.scipy.linalg.solve_triangular(lower_tri, right_rows.T, lower=True).T

def contribution(pivot_block, border, update):
    lower_tri = jnp.linalg.cholesky(pivot_block)
    factor = solve_rows(lower_tri, border)
    return update - jnp.dot(factor.astype(jnp.float32), factor.T.astype(jnp.float32), precision=highest, preferred_element_type=jnp.float32)

def reference(child_pivot, child_border, child_update, parent_front, tile_map):
    offsets = jnp.arange(TILE, dtype=jnp.int32)
    parent = parent_front
    for member in range(CHILDREN):
        contrib = contribution(child_pivot[member], child_border[member], child_update[member])
        tile_ids = tile_map[member].astype(jnp.int32)
        indices = (tile_ids[:, None] * TILE + offsets[None, :]).reshape(-1)
        indices = jnp.where(indices >= 0, indices, PARENT).astype(jnp.int32)
        parent = parent.at[indices[:, None], indices[None, :]].add(contrib, mode='drop')
    top_lower = jnp.linalg.cholesky(parent[:PANEL, :PANEL])
    panel_rows = solve_rows(top_lower, parent[:, :PANEL])
    schur_block = parent - jnp.dot(panel_rows.astype(jnp.float32), panel_rows.T.astype(jnp.float32), precision=highest, preferred_element_type=jnp.float32)
    return (schur_block, panel_rows)
```

```python
import jax
import jax.numpy as jnp
from jax import lax
from jax.experimental import pallas as pl
from jax.experimental.pallas import tpu as pltpu
from jax.sharding import Mesh, PartitionSpec as P

PANEL = 256
TILE = 128
AXES = ("y", "zl", "x", "zh", "core")
SIZES = (4, 2, 4, 4, 2)
ROW = ("x", "zh")
GRP = ("y", "zl", "core")
SUB = ("y", "zl")
LANES = 128

highest = lax.Precision.HIGHEST
VMEM = pl.BlockSpec(memory_space=pltpu.VMEM)
SMEM = pl.BlockSpec(memory_space=pltpu.SMEM)


def dot(a, b, ca=1, cb=0):
    return lax.dot_general(
        a, b, (((ca,), (cb,)), ((), ())), precision=highest, preferred_element_type=jnp.float32
    )


def inverse_factor_rows(groups):
    count = len(groups)
    full = (8, LANES)
    lane = lax.broadcasted_iota(jnp.int32, full, 1)
    sublane = lax.broadcasted_iota(jnp.int32, full, 0)
    d = list(groups)
    out = [None] * count
    for g in range(count):
        base = 8 * g
        inside = (lane >= base) & (lane < base + 8)
        own = d[g]
        cols = [jnp.broadcast_to(own[:, base + q : base + q + 1], full) for q in range(8)]
        e = [[None] * 8 for _ in range(8)]
        for q in range(8):
            for i in range(q, 8):
                e[i][q] = jnp.broadcast_to(cols[q][i : i + 1, :], full)
        y = []
        for i in range(8):
            row = jnp.broadcast_to(own[i : i + 1, :], full)
            y.append(jnp.where(inside, jnp.where(lane == base + i, 1.0, 0.0), row))
        inv = [None] * 8
        low = [[None] * 8 for _ in range(8)]
        for p in range(8):
            inv[p] = 1.0 / e[p][p]
            for i in range(p + 1, 8):
                low[i][p] = e[i][p] * inv[p]
            for i in range(p + 1, 8):
                for j in range(p + 1, i + 1):
                    e[i][j] = e[i][j] - low[i][p] * e[j][p]
                y[i] = y[i] - low[i][p] * y[p]
        rows = y[0] * lax.rsqrt(e[0][0])
        for i in range(1, 8):
            rows = jnp.where(sublane == i, y[i] * lax.rsqrt(e[i][i]), rows)
        out[g] = jnp.where(lane <= sublane + base, rows, 0.0)
        if g == count - 1:
            break
        s = [y[i] * inv[i] for i in range(8)]
        for i in range(6, -1, -1):
            for p in range(i + 1, 8):
                s[i] = s[i] - low[p][i] * s[p]
        for r in range(g + 1, count):
            acc = jnp.where(inside, 0.0, d[r])
            for q in range(8):
                acc = acc - jnp.broadcast_to(d[r][:, base + q : base + q + 1], full) * s[q]
            d[r] = acc
    return out


def inverse_factor_kernel(p_ref, x_ref, block_ref):
    n = x_ref.shape[0]
    steps = n // LANES
    if len(p_ref.shape) == 2:
        x_ref[...] = p_ref[...]
    else:
        halves, pieces, rows, _ = p_ref.shape
        for h in range(halves):
            for i in range(pieces):
                start = (i * halves + h) * rows
                x_ref[start : start + rows, :] = p_ref[h, i]
    square = (LANES, LANES)
    eye = (
        lax.broadcasted_iota(jnp.int32, square, 0) == lax.broadcasted_iota(jnp.int32, square, 1)
    ).astype(jnp.float32)

    def step(k, carry):
        k0 = pl.multiple_of(k * LANES, LANES)
        here = pl.ds(k0, LANES)
        groups = [x_ref[pl.ds(k0 + 8 * r, 8), here] for r in range(LANES // 8)]
        for r, rows in enumerate(inverse_factor_rows(groups)):
            block_ref[8 * r : 8 * r + 8, :] = rows
        x_ref[here, here] = eye
        block = block_ref[...]
        scaled = dot(block, x_ref[here, :])
        solved = dot(block, scaled, 0, 0)
        x_ref[here, :] = scaled

        def update(r, inner):
            there = pl.ds(pl.multiple_of(r * LANES, LANES), LANES)
            below = x_ref[there, here]
            x_ref[there, here] = jnp.zeros(square, jnp.float32)
            x_ref[there, :] = x_ref[there, :] - dot(below, solved)
            return inner

        lax.fori_loop(k + 1, steps, update, 0)
        return carry

    lax.fori_loop(0, steps, step, 0)
    row = lax.broadcasted_iota(jnp.int32, (LANES, n), 0)
    column = lax.broadcasted_iota(jnp.int32, (LANES, n), 1)

    def finish(k, carry):
        k0 = pl.multiple_of(k * LANES, LANES)
        x_ref[pl.ds(k0, LANES), :] = jnp.where(column <= row + k0, x_ref[pl.ds(k0, LANES), :], 0.0)
        return carry

    lax.fori_loop(0, steps, finish, 0)


def inverse_factor(block, n):
    return pl.pallas_call(
        inverse_factor_kernel,
        out_shape=jax.ShapeDtypeStruct((n, n), jnp.float32),
        in_specs=[VMEM],
        out_specs=VMEM,
        scratch_shapes=[pltpu.VMEM((LANES, LANES), jnp.float32)],
        compiler_params=pltpu.CompilerParams(vmem_limit_bytes=24 * 2**20),
        cost_estimate=pl.CostEstimate(flops=2 * n**3 * 6, bytes_accessed=8 * n * n, transcendentals=0),
        name="inverse_factor",
    )(block)


def contrib_kernel(w_ref, border_ref, update_ref, out_ref):
    pair, tile, depth = border_ref.shape
    product = dot(w_ref[...], border_ref[...].reshape(pair * tile, depth), 1, 1)
    for h in range(pair):
        out_ref[h] = update_ref[h] - product[:, h * tile : (h + 1) * tile]


def contributions(w, border, update):
    count, tile, depth = border.shape
    rows = w.shape[0]
    pair = 2
    return pl.pallas_call(
        contrib_kernel,
        grid=(count // pair,),
        out_shape=jax.ShapeDtypeStruct((count, rows, tile), jnp.float32),
        in_specs=[
            pl.BlockSpec((rows, depth), lambda j: (0, 0)),
            pl.BlockSpec((pair, tile, depth), lambda j: (j, 0, 0)),
            pl.BlockSpec((pair, rows, tile), lambda j: (j, 0, 0)),
        ],
        out_specs=pl.BlockSpec((pair, rows, tile), lambda j: (j, 0, 0)),
        compiler_params=pltpu.CompilerParams(vmem_limit_bytes=24 * 2**20),
        name="contributions",
    )(w, border, update)


def near_kernel(map_ref, at_ref, got_ref, base_ref, out_ref):
    i = at_ref[0]
    offset = got_ref.shape[1] - 16
    out_ref[...] = base_ref[...]
    for s in range(map_ref.shape[0]):
        for c in range(2):
            cb = map_ref[s, c]
            for a in range(2):
                ra = map_ref[s, 2 * i + a]

                @pl.when((ra >= 0) & (cb >= 0) & (cb < PANEL // TILE))
                def _():
                    rows = pl.ds(pl.multiple_of((ra - 8 * i) * 8, 8), 8)
                    lanes = pl.ds(pl.multiple_of(cb * TILE, TILE), TILE)
                    piece = got_ref[2 * s + c, offset + 8 * a : offset + 8 * a + 8, :]
                    out_ref[rows, lanes] = out_ref[rows, lanes] + piece


def assemble_kernel(map_ref, at_ref, got_ref, parent_ref, out_ref):
    i = at_ref[0]
    g = at_ref[1]
    out_ref[...] = parent_ref[...]
    for s in range(map_ref.shape[0]):
        for c in range(2):
            cb = map_ref[s, 2 * g + c]
            for a in range(2):
                ra = map_ref[s, 2 * i + a]

                @pl.when((ra >= 0) & (cb >= 0))
                def _():
                    rows = pl.ds(pl.multiple_of((ra - 8 * i) * TILE, TILE), TILE)
                    lanes = pl.ds(pl.multiple_of((cb - 8 * g) * TILE, TILE), TILE)
                    piece = got_ref[2 * s + c, TILE * a : TILE * a + TILE, :]
                    out_ref[rows, lanes] = out_ref[rows, lanes] + piece


def placed_sum(kernel, name, tile_map, at, got, base):
    return pl.pallas_call(
        kernel,
        out_shape=jax.ShapeDtypeStruct(base.shape, jnp.float32),
        in_specs=[SMEM, SMEM, VMEM, VMEM],
        out_specs=VMEM,
        compiler_params=pltpu.CompilerParams(vmem_limit_bytes=24 * 2**20),
        name=name,
    )(tile_map, at, got, base)


def gathered(value, axis):
    peers = lax.axis_size(axis)
    copies = jnp.broadcast_to(value[None], (peers, *value.shape))
    return lax.all_to_all(copies, axis, 0, 0, tiled=True)


def transposed_pairs():
    pairs = []
    for r in range(16):
        for k in range(16):

            def flat(row, group):
                x, zh = divmod(row, 4)
                y, rest = divmod(group, 4)
                zl, core = divmod(rest, 2)
                return (((y * 2 + zl) * 4 + x) * 4 + zh) * 2 + core

            pairs.append((flat(r, k), flat(k, r)))
    return pairs


def slices_to_rows(slices):
    count, rows, cols = slices.shape
    tiles = rows // 8
    return slices.reshape(count, tiles, 8, cols).transpose(1, 0, 2, 3).reshape(count * rows, cols)


def rows_to_slices(rows, count):
    total, cols = rows.shape
    tiles = total // (8 * count)
    return rows.reshape(tiles, count, 8, cols).transpose(1, 0, 2, 3).reshape(count, tiles * 8, cols)


def on_device(child_pivot, child_border, child_update, parent_front, tile_map):
    core = lax.axis_index("core")
    row = lax.axis_index(ROW)
    group = lax.axis_index(GRP)
    at = jnp.stack([row, group]).astype(jnp.int32)
    border = child_border[0]

    part = lax.dynamic_slice_in_dim(child_pivot[0], core * 32, 32, 0)
    pivot = gathered(gathered(gathered(part, "zh"), "x"), "core")
    pivot = pivot.reshape(2, 16, 32, pivot.shape[-1])

    half = lax.dynamic_slice_in_dim(border, core * TILE, TILE, 0)
    far_border = lax.all_gather(half, ROW, axis=0, tiled=False)

    update = child_update[0].reshape(256, 8, 2, TILE).transpose(2, 1, 0, 3)
    update = lax.all_to_all(update, "core", 0, 0, tiled=True).reshape(16, 256, TILE)

    base = lax.all_to_all(rows_to_slices(parent_front[:, :PANEL], 16), GRP, 0, 0, tiled=True)[0]

    inverse = inverse_factor(pivot, pivot.shape[-1])
    solved = dot(dot(border, inverse, 1, 1), inverse)
    contrib = contributions(solved, far_border, update)
    send = jnp.concatenate([contrib, rows_to_slices(contrib[0], 16)], axis=1)
    got = lax.all_to_all(send, GRP, 0, 0, tiled=True)

    mine = placed_sum(near_kernel, "near", tile_map, at, got, base)
    top = gathered(gathered(mine[:16], "x")[0], "zh")[0]
    far = lax.ppermute(mine, AXES, transposed_pairs())
    both = gathered(jnp.concatenate([mine, top], axis=0), GRP)
    parent = placed_sum(assemble_kernel, "assemble", tile_map, at, got, parent_front)
    near = slices_to_rows(both[:, :64])
    top_block = slices_to_rows(both[:, 64:])
    far = gathered(gathered(far, "zh"), "x").reshape(16, 64, PANEL)
    far = slices_to_rows(far)

    top_inverse = inverse_factor(top_block, PANEL)
    panel_rows = dot(near, top_inverse, 1, 1)
    far_rows = dot(far, top_inverse, 1, 1)
    schur_block = parent - dot(panel_rows, far_rows, 1, 1)
    return (schur_block, panel_rows)


def solution(mesh):
    fine = Mesh(mesh.devices.reshape(SIZES), AXES)
    placed = (
        P(SUB, ROW, None),
        P(SUB, ROW, None),
        P(SUB, ROW, "core"),
        P(ROW, GRP),
        P(),
    )
    return jax.shard_map(
        on_device,
        mesh=fine,
        in_specs=placed,
        out_specs=(P(ROW, GRP), P(ROW, None)),
        check_vma=False,
    )
```

```python
import functools

import jax
import jax.numpy as jnp
from jax import lax
from jax.experimental import pallas as pl
from jax.experimental.pallas import tpu as pltpu
from jax.sharding import Mesh, PartitionSpec as P

PANEL = 256
TILE = 128
AXES = ("y", "zl", "x", "zh", "core")
SIZES = (4, 2, 4, 4, 2)
ROW = ("x", "zh")
GRP = ("y", "zl", "core")
SUB = ("y", "zl")
LANES = 128

highest = lax.Precision.HIGHEST
VMEM = pl.BlockSpec(memory_space=pltpu.VMEM)
SMEM = pl.BlockSpec(memory_space=pltpu.SMEM)


def dot(a, b, ca=1, cb=0):
    return lax.dot_general(
        a, b, (((ca,), (cb,)), ((), ())), precision=highest, preferred_element_type=jnp.float32
    )


def halves_of(value):
    high = value.astype(jnp.bfloat16)
    return high, (value - high.astype(jnp.float32)).astype(jnp.bfloat16)


def split_dot(a, b):
    a_high, a_low = halves_of(a)
    b_high, b_low = halves_of(b)
    part = lambda p, q: lax.dot_general(
        p, q, (((1,), (1,)), ((), ())), preferred_element_type=jnp.float32
    )
    return part(a_high, b_high) + (part(a_high, b_low) + part(a_low, b_high))


def inverse_factor_rows(groups):
    count = len(groups)
    full = (8, LANES)
    lane = lax.broadcasted_iota(jnp.int32, full, 1)
    sublane = lax.broadcasted_iota(jnp.int32, full, 0)
    d = list(groups)
    out = [None] * count
    for g in range(count):
        base = 8 * g
        inside = (lane >= base) & (lane < base + 8)
        own = d[g]
        cols = [jnp.broadcast_to(own[:, base + q : base + q + 1], full) for q in range(8)]
        e = [[None] * 8 for _ in range(8)]
        for q in range(8):
            for i in range(q, 8):
                e[i][q] = jnp.broadcast_to(cols[q][i : i + 1, :], full)
        y = []
        for i in range(8):
            row = jnp.broadcast_to(own[i : i + 1, :], full)
            y.append(jnp.where(inside, jnp.where(lane == base + i, 1.0, 0.0), row))
        inv = [None] * 8
        low = [[None] * 8 for _ in range(8)]
        for p in range(8):
            inv[p] = 1.0 / e[p][p]
            for i in range(p + 1, 8):
                low[i][p] = e[i][p] * inv[p]
            for i in range(p + 1, 8):
                for j in range(p + 1, i + 1):
                    e[i][j] = e[i][j] - low[i][p] * e[j][p]
                y[i] = y[i] - low[i][p] * y[p]
        rows = y[0] * lax.rsqrt(e[0][0])
        for i in range(1, 8):
            rows = jnp.where(sublane == i, y[i] * lax.rsqrt(e[i][i]), rows)
        out[g] = jnp.where(lane <= sublane + base, rows, 0.0)
        if g == count - 1:
            break
        s = [y[i] * inv[i] for i in range(8)]
        for i in range(6, -1, -1):
            for p in range(i + 1, 8):
                s[i] = s[i] - low[p][i] * s[p]
        for r in range(g + 1, count):
            acc = jnp.where(inside, 0.0, d[r])
            for q in range(8):
                acc = acc - jnp.broadcast_to(d[r][:, base + q : base + q + 1], full) * s[q]
            d[r] = acc
    return out


def eliminate(x_ref, s_ref, block_ref, first, last):
    n = x_ref.shape[0]
    steps = n // LANES
    square = (LANES, LANES)
    eye = (
        lax.broadcasted_iota(jnp.int32, square, 0) == lax.broadcasted_iota(jnp.int32, square, 1)
    ).astype(jnp.float32)

    def step(k, carry):
        k0 = pl.multiple_of(k * LANES, LANES)
        here = pl.ds(k0, LANES)
        groups = [x_ref[pl.ds(k0 + 8 * r, 8), here] for r in range(LANES // 8)]
        for r, rows in enumerate(inverse_factor_rows(groups)):
            block_ref[8 * r : 8 * r + 8, :] = rows
        x_ref[here, here] = eye
        block = block_ref[...]
        scaled = dot(block, x_ref[here, :])
        solved = dot(block, scaled, 0, 0)
        x_ref[here, :] = scaled
        s_ref[here, :] = solved

        def update(r, inner):
            there = pl.ds(pl.multiple_of(r * LANES, LANES), LANES)
            below = x_ref[there, here]
            x_ref[there, here] = jnp.zeros(square, jnp.float32)
            x_ref[there, :] = x_ref[there, :] - dot(below, solved)
            return inner

        lax.fori_loop(k + 1, steps, update, 0)
        return carry

    lax.fori_loop(first, last, step, 0)


def open_kernel(last, at_ref, own_ref, other_ref, x_ref, s_ref, block_ref):
    core = at_ref[2]
    pieces, rows, _ = own_ref.shape
    for i in range(pieces):
        start = i * 2 * rows
        x_ref[pl.ds(pl.multiple_of(start + core * rows, rows), rows), :] = own_ref[i]
        x_ref[pl.ds(pl.multiple_of(start + (1 - core) * rows, rows), rows), :] = other_ref[i]
    eliminate(x_ref, s_ref, block_ref, 0, last)


def close_kernel(first, x_in, s_in, x_ref, s_ref, block_ref):
    del x_in, s_in
    eliminate(x_ref, s_ref, block_ref, first, x_ref.shape[0] // LANES)


def elimination(at, own, other, n, split):
    shape = jax.ShapeDtypeStruct((n, n), jnp.float32)
    common = dict(
        out_shape=(shape, shape),
        out_specs=(VMEM, VMEM),
        scratch_shapes=[pltpu.VMEM((LANES, LANES), jnp.float32)],
        compiler_params=pltpu.CompilerParams(vmem_limit_bytes=10 * 2**20),
    )
    cost = lambda share: pl.CostEstimate(
        flops=int(share * 40e9), bytes_accessed=8 * n * n, transcendentals=0
    )
    state = pl.pallas_call(
        functools.partial(open_kernel, split), in_specs=[SMEM, VMEM, VMEM], cost_estimate=cost(0.66), name="open_factor", **common
    )(at, own, other)
    return lambda x, s: pl.pallas_call(
        functools.partial(close_kernel, split),
        in_specs=[VMEM, VMEM],
        input_output_aliases={0: 0, 1: 1},
        cost_estimate=cost(0.34),
        name="close_factor",
        **common,
    )(x, s)[1], state


OFFSETS = (0, -1, 1, 2)


def contrib_kernel(at_ref, s_ref, own_ref, h_ref, up_ref, down_ref, far0_ref, far1_ref, keep_ref, sent_ref, out_ref, w_ref):
    core, x, zh = at_ref[2], at_ref[3], at_ref[4]
    depth = s_ref.shape[0]
    rows = own_ref.shape[0]
    w_ref[...] = own_ref[...]
    for k in range(depth // LANES):
        lanes = slice(k * LANES, (k + 1) * LANES)
        pivot = w_ref[:, lanes]
        w_ref[:, lanes] = jnp.zeros((rows, LANES), jnp.float32)
        w_ref[...] = w_ref[...] - dot(pivot, s_ref[lanes, :])
    pairs = []
    for ref, dx in ((h_ref, 0), (up_ref, -1), (down_ref, 1)):
        pairs += [(ref, 0, dx, 0), (ref, 2, dx, 2)]
    pairs += [(far0_ref, 0, 2, 0), (far1_ref, 0, 2, 2)]
    for ref, start, dx, dz in pairs:
        block = ref[start : start + 2].reshape(2 * TILE, depth)
        product = dot(w_ref[...], block, 1, 1)
        for t in range(2):
            j = ((x + dx) & 3) * 4 + ((zh + OFFSETS[dz + t]) & 3)
            mine = (j // 8) == core
            inner = j % 8
            u = jnp.where(mine, keep_ref[inner], sent_ref[inner])
            out_ref[j, 0:rows, :] = u + product[:, t * TILE : (t + 1) * TILE]
    for k in range(16):
        for a in range(2):
            out_ref[k, rows + 8 * a : rows + 8 * a + 8, :] = out_ref[
                0, a * TILE + 8 * k : a * TILE + 8 * k + 8, :
            ]


def contributions(at, solved, border, pieces, keep, sent):
    rows = border.shape[0]
    return pl.pallas_call(
        contrib_kernel,
        out_shape=jax.ShapeDtypeStruct((16, rows + 16, TILE), jnp.float32),
        in_specs=[SMEM] + [VMEM] * 9,
        out_specs=VMEM,
        scratch_shapes=[pltpu.VMEM(border.shape, jnp.float32)],
        compiler_params=pltpu.CompilerParams(vmem_limit_bytes=10 * 2**20),
        name="contributions",
    )(at, solved, border, *pieces, keep, sent)


def split_kernel(at_ref, u_ref, keep_ref, send_ref):
    core = at_ref[2]
    for m in range(keep_ref.shape[0]):
        keep_ref[m] = u_ref[:, pl.ds(pl.multiple_of((2 * m + core) * TILE, TILE), TILE)]
        send_ref[m] = u_ref[:, pl.ds(pl.multiple_of((2 * m + 1 - core) * TILE, TILE), TILE)]


def split_update(at, update):
    rows, cols = update.shape
    shape = jax.ShapeDtypeStruct((cols // (2 * TILE), rows, TILE), jnp.float32)
    return pl.pallas_call(
        split_kernel,
        out_shape=(shape, shape),
        in_specs=[SMEM, VMEM],
        out_specs=(VMEM, VMEM),
        name="split_update",
    )(at, update)


def panel_kernel(both_ref, panel_ref, x_ref, s_ref, block_ref, rows_ref):
    near = rows_ref.shape[0] // TILE
    for k in range(both_ref.shape[0]):
        for a in range(both_ref.shape[1] // 8):
            to, at = (rows_ref, a) if a < near else (x_ref, a - near)
            to[at * TILE + 8 * k : at * TILE + 8 * k + 8, :] = both_ref[k, 8 * a : 8 * a + 8, :]
    n = x_ref.shape[0]
    eliminate(x_ref, s_ref, block_ref, 0, n // LANES)
    row = lax.broadcasted_iota(jnp.int32, (n, n), 0)
    column = lax.broadcasted_iota(jnp.int32, (n, n), 1)
    x_ref[...] = jnp.where(column <= row, x_ref[...], 0.0)
    panel_ref[...] = dot(rows_ref[...], x_ref[...], 1, 1)


def panel(both):
    pieces, height, n = both.shape
    rows = pieces * height - n
    return pl.pallas_call(
        panel_kernel,
        out_shape=(jax.ShapeDtypeStruct((rows, n), jnp.float32), jax.ShapeDtypeStruct((n, n), jnp.float32)),
        in_specs=[VMEM],
        out_specs=(VMEM, VMEM),
        scratch_shapes=[
            pltpu.VMEM((n, n), jnp.float32),
            pltpu.VMEM((LANES, LANES), jnp.float32),
            pltpu.VMEM((rows, n), jnp.float32),
        ],
        cost_estimate=pl.CostEstimate(flops=int(8e9), bytes_accessed=3 * 2**20, transcendentals=0),
        compiler_params=pltpu.CompilerParams(vmem_limit_bytes=10 * 2**20),
        name="panel",
    )(both)


def schur_kernel(at_ref, parent_ref, panel_ref, x_ref, *refs):
    far_refs = refs[:4]
    out_ref, rows_ref, solved_ref = refs[4:]
    x, zh = at_ref[3], at_ref[4]
    r = pl.program_id(0)

    @pl.when(r == 0)
    def _():
        for dx, far_ref in enumerate(far_refs):
            for dz in range(4):
                k = (x ^ dx) * 4 + (zh ^ dz)
                for a in range(far_ref.shape[1] // 8):
                    rows_ref[pl.ds(pl.multiple_of(a * TILE + 8 * k, 8), 8), :] = far_ref[
                        dz, 8 * a : 8 * a + 8, :
                    ]
        solved_ref[...] = dot(rows_ref[...], x_ref[...], 1, 1)

    step = out_ref.shape[0]
    here = pl.ds(pl.multiple_of(r * step, step), step)
    out_ref[...] = parent_ref[here, :] - split_dot(panel_ref[here, :], solved_ref[...])


def schur(at, parent, panel_rows, inverse, far):
    rows, cols = parent.shape
    n = panel_rows.shape[1]
    step = 256
    return pl.pallas_call(
        schur_kernel,
        grid=(rows // step,),
        out_shape=jax.ShapeDtypeStruct(parent.shape, jnp.float32),
        in_specs=[SMEM] + [VMEM] * 7,
        out_specs=pl.BlockSpec((step, cols), lambda r: (r, 0)),
        scratch_shapes=[pltpu.VMEM((rows, n), jnp.float32), pltpu.VMEM((rows, n), jnp.float32)],
        compiler_params=pltpu.CompilerParams(vmem_limit_bytes=16 * 2**20),
        name="schur",
    )(at, parent, panel_rows, inverse, *far)


def near_kernel(map_ref, at_ref, got_ref, base_ref, out_ref):
    i = at_ref[0]
    offset = got_ref.shape[1] - 16
    out_ref[...] = base_ref[...]
    for s in range(map_ref.shape[0]):
        for c in range(2):
            cb = map_ref[s, c]
            for a in range(2):
                ra = map_ref[s, 2 * i + a]

                @pl.when((ra >= 0) & (cb >= 0) & (cb < PANEL // TILE))
                def _():
                    rows = pl.ds(pl.multiple_of((ra - 8 * i) * 8, 8), 8)
                    lanes = pl.ds(pl.multiple_of(cb * TILE, TILE), TILE)
                    piece = got_ref[2 * s + c, offset + 8 * a : offset + 8 * a + 8, :]
                    out_ref[rows, lanes] = out_ref[rows, lanes] + piece


def assemble_kernel(map_ref, at_ref, got_ref, parent_ref, out_ref):
    i = at_ref[0]
    g = at_ref[1]
    out_ref[...] = parent_ref[...]
    for s in range(map_ref.shape[0]):
        for c in range(2):
            cb = map_ref[s, 2 * g + c]
            for a in range(2):
                ra = map_ref[s, 2 * i + a]

                @pl.when((ra >= 0) & (cb >= 0))
                def _():
                    rows = pl.ds(pl.multiple_of((ra - 8 * i) * TILE, TILE), TILE)
                    lanes = pl.ds(pl.multiple_of((cb - 8 * g) * TILE, TILE), TILE)
                    piece = got_ref[2 * s + c, TILE * a : TILE * a + TILE, :]
                    out_ref[rows, lanes] = out_ref[rows, lanes] + piece


def placed_sum(kernel, name, tile_map, at, got, base):
    return pl.pallas_call(
        kernel,
        out_shape=jax.ShapeDtypeStruct(base.shape, jnp.float32),
        in_specs=[SMEM, SMEM, VMEM, VMEM],
        out_specs=VMEM,
        compiler_params=pltpu.CompilerParams(vmem_limit_bytes=10 * 2**20),
        name=name,
    )(tile_map, at, got, base)


def gathered(value, axis):
    peers = lax.axis_size(axis)
    copies = jnp.broadcast_to(value[None], (peers, *value.shape))
    return lax.all_to_all(copies, axis, 0, 0, tiled=True)


def transposed_pairs():
    pairs = []
    for r in range(16):
        for k in range(16):

            def flat(row, group):
                x, zh = divmod(row, 4)
                y, rest = divmod(group, 4)
                zl, core = divmod(rest, 2)
                return (((y * 2 + zl) * 4 + x) * 4 + zh) * 2 + core

            pairs.append((flat(r, k), flat(k, r)))
    return pairs


def shifted(value, axis, by):
    peers = lax.axis_size(axis)
    return lax.ppermute(value, axis, [(i, (i + by) % peers) for i in range(peers)])


def ring_pieces(value, axis):
    middle = value.shape[0] // 2
    up = shifted(value, axis, 1)
    down = shifted(value, axis, -1)
    return up, down, shifted(up[:middle], axis, 1), shifted(down[middle:], axis, -1)


def flipped(value, axis):
    return [value] + [
        lax.ppermute(value, axis, [(i, i ^ by) for i in range(4)]) for by in (1, 2, 3)
    ]


def rows_to_slices(rows, count):
    total, cols = rows.shape
    tiles = total // (8 * count)
    return rows.reshape(tiles, count, 8, cols).transpose(1, 0, 2, 3).reshape(count, tiles * 8, cols)


def on_device(child_pivot, child_border, child_update, parent_front, tile_map):
    core = lax.axis_index("core")
    row = lax.axis_index(ROW)
    group = lax.axis_index(GRP)
    at = jnp.stack([row, group, core, lax.axis_index("x"), lax.axis_index("zh")]).astype(jnp.int32)
    border = child_border[0]
    n = child_pivot.shape[-1]

    part = lax.dynamic_slice_in_dim(child_pivot[0], core * 32, 32, 0)
    pivot = gathered(part, "zh")
    half = lax.dynamic_slice_in_dim(border, core * TILE, TILE, 0)
    corner = rows_to_slices(parent_front[:, :PANEL], 16).reshape(4, 2, 2, 64, PANEL)
    quarters = [lax.ppermute(corner[q], GRP, [(0, 4 * q)]) for q in (1, 2, 3)]
    corner = jnp.where(lax.axis_index("y") == 0, corner[0], quarters[0] + quarters[1] + quarters[2])
    pivot, half, update, corner = lax.optimization_barrier((pivot, half, child_update[0], corner))
    up, down, far0, far1 = ring_pieces(half, "zh")
    column = jnp.stack([half, up, down, jnp.concatenate([far0, far1], axis=0)])
    pivot = gathered(pivot, "x")
    keep, send = split_update(at, update)
    sent = lax.ppermute(send, "core", [(0, 1), (1, 0)])
    eighth = lax.ppermute(corner[1], GRP, [(4 * y, 4 * y + 2) for y in range(4)])
    corner = jnp.where(lax.axis_index("zl") == 0, corner[0], eighth)
    pivot, corner, keep, sent, column = lax.optimization_barrier((pivot, corner, keep, sent, column))
    pivot = pivot.reshape(16, 32, n)
    other = lax.ppermute(pivot, "core", [(0, 1), (1, 0)])
    last = lax.ppermute(corner[1], GRP, [(2 * m, 2 * m + 1) for m in range(8)])
    base = jnp.where(core == 0, corner[0], last)

    split = 5
    close, state = elimination(at, pivot, other, n, split)
    up = shifted(column, "x", 1)
    down = shifted(column, "x", -1)
    x_state, s_state, up, down = lax.optimization_barrier((*state, up, down))
    far0 = shifted(up[:2], "x", 1)
    far1 = shifted(down[2:], "x", -1)
    solved = close(x_state, s_state)
    send = contributions(at, solved, border, (column, up, down, far0, far1), keep, sent)
    got = lax.all_to_all(send, GRP, 0, 0, tiled=True)

    mine = placed_sum(near_kernel, "near", tile_map, at, got, base)
    far = lax.ppermute(mine, AXES, transposed_pairs())
    top = gathered(gathered(mine[:16], "x")[0], "zh")[0]
    top, far = lax.optimization_barrier((top, far))
    far = jnp.stack(flipped(far, "zh"))
    both = gathered(jnp.concatenate([mine, top], axis=0), GRP)
    parent = placed_sum(assemble_kernel, "assemble", tile_map, at, got, parent_front)
    both, far, parent = lax.optimization_barrier((both, far, parent))
    far = flipped(far, "x")
    panel_rows, inverse = panel(both)
    schur_block = schur(at, parent, panel_rows, inverse, far)
    return (schur_block, panel_rows)


def solution(mesh):
    fine = Mesh(mesh.devices.reshape(SIZES), AXES)
    placed = (
        P(SUB, ROW, None),
        P(SUB, ROW, None),
        P(SUB, ROW, "core"),
        P(ROW, GRP),
        P(),
    )
    return jax.shard_map(
        on_device,
        mesh=fine,
        in_specs=placed,
        out_specs=(P(ROW, GRP), P(ROW, None)),
        check_vma=False,
    )
```

```python
import functools

import jax
import jax.numpy as jnp
from jax import lax
from jax.experimental import pallas as pl
from jax.experimental.pallas import tpu as pltpu
from jax.sharding import Mesh, PartitionSpec as P

PANEL = 256
TILE = 128
AXES = ("y", "zl", "x", "zh", "core")
SIZES = (4, 2, 4, 4, 2)
ROW = ("x", "zh")
GRP = ("y", "zl", "core")
SUB = ("y", "zl")
LANES = 128

highest = lax.Precision.HIGHEST
VMEM = pl.BlockSpec(memory_space=pltpu.VMEM)
SMEM = pl.BlockSpec(memory_space=pltpu.SMEM)


def dot(a, b, ca=1, cb=0):
    return lax.dot_general(
        a, b, (((ca,), (cb,)), ((), ())), precision=highest, preferred_element_type=jnp.float32
    )


def halves_of(value):
    high = value.astype(jnp.bfloat16)
    return high, (value - high.astype(jnp.float32)).astype(jnp.bfloat16)


def thirds_of(value):
    high = value.astype(jnp.bfloat16)
    rest = value - high.astype(jnp.float32)
    middle = rest.astype(jnp.bfloat16)
    return high, middle, (rest - middle.astype(jnp.float32)).astype(jnp.bfloat16)


def left_parts(value):
    high, middle, low = thirds_of(value)
    return jnp.concatenate([high, middle, high, middle, high, low], axis=1)


def right_parts(value):
    high, middle, low = thirds_of(value)
    return jnp.concatenate([high, high, middle, middle, low, high], axis=0)


def parts_dot(left, right):
    return lax.dot_general(
        left, right, (((1,), (0,)), ((), ())), preferred_element_type=jnp.float32
    )


def split_dot(a, b):
    a_high, a_low = halves_of(a)
    b_high, b_low = halves_of(b)
    part = lambda p, q: lax.dot_general(
        p, q, (((1,), (1,)), ((), ())), preferred_element_type=jnp.float32
    )
    return part(a_high, b_high) + (part(a_high, b_low) + part(a_low, b_high))


def inverse_factor_rows(groups):
    count = len(groups)
    full = (8, LANES)
    lane = lax.broadcasted_iota(jnp.int32, full, 1)
    sublane = lax.broadcasted_iota(jnp.int32, full, 0)
    d = list(groups)
    out = [None] * count
    for g in range(count):
        base = 8 * g
        inside = (lane >= base) & (lane < base + 8)
        own = d[g]
        cols = [jnp.broadcast_to(own[:, base + q : base + q + 1], full) for q in range(8)]
        e = [[None] * 8 for _ in range(8)]
        for q in range(8):
            for i in range(q, 8):
                e[i][q] = jnp.broadcast_to(cols[q][i : i + 1, :], full)
        y = []
        for i in range(8):
            row = jnp.broadcast_to(own[i : i + 1, :], full)
            y.append(jnp.where(inside, jnp.where(lane == base + i, 1.0, 0.0), row))
        inv = [None] * 8
        low = [[None] * 8 for _ in range(8)]
        for p in range(8):
            inv[p] = 1.0 / e[p][p]
            for i in range(p + 1, 8):
                low[i][p] = e[i][p] * inv[p]
            for i in range(p + 1, 8):
                for j in range(p + 1, i + 1):
                    e[i][j] = e[i][j] - low[i][p] * e[j][p]
                y[i] = y[i] - low[i][p] * y[p]
        rows = y[0] * lax.rsqrt(e[0][0])
        for i in range(1, 8):
            rows = jnp.where(sublane == i, y[i] * lax.rsqrt(e[i][i]), rows)
        out[g] = jnp.where(lane <= sublane + base, rows, 0.0)
        if g == count - 1:
            break
        s = [y[i] * inv[i] for i in range(8)]
        for i in range(6, -1, -1):
            for p in range(i + 1, 8):
                s[i] = s[i] - low[p][i] * s[p]
        for r in range(g + 1, count):
            acc = jnp.where(inside, 0.0, d[r])
            for q in range(8):
                acc = acc - jnp.broadcast_to(d[r][:, base + q : base + q + 1], full) * s[q]
            d[r] = acc
    return out


def eliminate(x_ref, s_ref, block_ref, parts_ref, first, last):
    n = x_ref.shape[0]
    steps = n // LANES
    square = (LANES, LANES)
    eye = (
        lax.broadcasted_iota(jnp.int32, square, 0) == lax.broadcasted_iota(jnp.int32, square, 1)
    ).astype(jnp.float32)

    def step(k, carry):
        k0 = pl.multiple_of(k * LANES, LANES)
        here = pl.ds(k0, LANES)
        groups = [x_ref[pl.ds(k0 + 8 * r, 8), here] for r in range(LANES // 8)]
        for r, rows in enumerate(inverse_factor_rows(groups)):
            block_ref[8 * r : 8 * r + 8, :] = rows
        x_ref[here, here] = eye
        block = block_ref[...]
        scaled = dot(block, x_ref[here, :])
        solved = dot(block, scaled, 0, 0)
        x_ref[here, :] = scaled
        s_ref[here, :] = solved
        parts_ref[...] = right_parts(solved)

        def update(r, inner):
            there = pl.ds(pl.multiple_of(r * LANES, LANES), LANES)
            below = x_ref[there, here]
            x_ref[there, here] = jnp.zeros(square, jnp.float32)
            x_ref[there, :] = x_ref[there, :] - parts_dot(left_parts(below), parts_ref[...])
            return inner

        lax.fori_loop(k + 1, steps, update, 0)
        return carry

    lax.fori_loop(first, last, step, 0)


def open_kernel(last, at_ref, own_ref, other_ref, x_ref, s_ref, block_ref, parts_ref):
    core = at_ref[2]
    pieces, rows, _ = own_ref.shape
    for i in range(pieces):
        start = i * 2 * rows
        x_ref[pl.ds(pl.multiple_of(start + core * rows, rows), rows), :] = own_ref[i]
        x_ref[pl.ds(pl.multiple_of(start + (1 - core) * rows, rows), rows), :] = other_ref[i]
    eliminate(x_ref, s_ref, block_ref, parts_ref, 0, last)


def close_kernel(first, x_in, s_in, x_ref, s_ref, block_ref, parts_ref):
    del x_in, s_in
    eliminate(x_ref, s_ref, block_ref, parts_ref, first, x_ref.shape[0] // LANES)


def elimination(at, own, other, n, split):
    shape = jax.ShapeDtypeStruct((n, n), jnp.float32)
    common = dict(
        out_shape=(shape, shape),
        out_specs=(VMEM, VMEM),
        scratch_shapes=[
            pltpu.VMEM((LANES, LANES), jnp.float32),
            pltpu.VMEM((6 * LANES, n), jnp.bfloat16),
        ],
        compiler_params=pltpu.CompilerParams(vmem_limit_bytes=10 * 2**20),
    )
    cost = lambda share: pl.CostEstimate(
        flops=int(share * 40e9), bytes_accessed=8 * n * n, transcendentals=0
    )
    state = pl.pallas_call(
        functools.partial(open_kernel, split), in_specs=[SMEM, VMEM, VMEM], cost_estimate=cost(0.66), name="open_factor", **common
    )(at, own, other)
    return lambda x, s: pl.pallas_call(
        functools.partial(close_kernel, split),
        in_specs=[VMEM, VMEM],
        input_output_aliases={0: 0, 1: 1},
        cost_estimate=cost(0.34),
        name="close_factor",
        **common,
    )(x, s)[1], state


OFFSETS = (0, -1, 1, 2)


def contrib_kernel(at_ref, s_ref, own_ref, h_ref, up_ref, down_ref, far0_ref, far1_ref, keep_ref, sent_ref, out_ref, w_ref):
    core, x, zh = at_ref[2], at_ref[3], at_ref[4]
    depth = s_ref.shape[0]
    rows = own_ref.shape[0]
    w_ref[...] = own_ref[...]

    def step(k, carry):
        here = pl.ds(pl.multiple_of(k * LANES, LANES), LANES)
        pivot = w_ref[:, here]
        w_ref[:, here] = jnp.zeros((rows, LANES), jnp.float32)
        w_ref[...] = w_ref[...] - parts_dot(left_parts(pivot), right_parts(s_ref[here, :]))
        return carry

    lax.fori_loop(0, depth // LANES, step, 0)
    pairs = []
    for ref, dx in ((h_ref, 0), (up_ref, -1), (down_ref, 1)):
        pairs += [(ref, 0, dx, 0), (ref, 2, dx, 2)]
    pairs += [(far0_ref, 0, 2, 0), (far1_ref, 0, 2, 2)]
    for ref, start, dx, dz in pairs:
        block = ref[start : start + 2].reshape(2 * TILE, depth)
        product = dot(w_ref[...], block, 1, 1)
        for t in range(2):
            j = ((x + dx) & 3) * 4 + ((zh + OFFSETS[dz + t]) & 3)
            mine = (j // 8) == core
            inner = j % 8
            u = jnp.where(mine, keep_ref[inner], sent_ref[inner])
            out_ref[j, 0:rows, :] = u + product[:, t * TILE : (t + 1) * TILE]
    for k in range(16):
        for a in range(2):
            out_ref[k, rows + 8 * a : rows + 8 * a + 8, :] = out_ref[
                0, a * TILE + 8 * k : a * TILE + 8 * k + 8, :
            ]


def contributions(at, solved, border, pieces, keep, sent):
    rows = border.shape[0]
    return pl.pallas_call(
        contrib_kernel,
        out_shape=jax.ShapeDtypeStruct((16, rows + 16, TILE), jnp.float32),
        in_specs=[SMEM] + [VMEM] * 9,
        out_specs=VMEM,
        scratch_shapes=[pltpu.VMEM(border.shape, jnp.float32)],
        compiler_params=pltpu.CompilerParams(vmem_limit_bytes=10 * 2**20),
        name="contributions",
    )(at, solved, border, *pieces, keep, sent)


def split_kernel(at_ref, u_ref, keep_ref, send_ref):
    core = at_ref[2]
    for m in range(keep_ref.shape[0]):
        keep_ref[m] = u_ref[:, pl.ds(pl.multiple_of((2 * m + core) * TILE, TILE), TILE)]
        send_ref[m] = u_ref[:, pl.ds(pl.multiple_of((2 * m + 1 - core) * TILE, TILE), TILE)]


def split_update(at, update):
    rows, cols = update.shape
    shape = jax.ShapeDtypeStruct((cols // (2 * TILE), rows, TILE), jnp.float32)
    return pl.pallas_call(
        split_kernel,
        out_shape=(shape, shape),
        in_specs=[SMEM, VMEM],
        out_specs=(VMEM, VMEM),
        name="split_update",
    )(at, update)


def panel_kernel(top_ref, near_ref, panel_ref, x_ref, s_ref, block_ref, parts_ref, rows_ref):
    for source, to in ((top_ref, x_ref), (near_ref, rows_ref)):
        for k in range(source.shape[0]):
            for a in range(source.shape[1] // 8):
                to[a * TILE + 8 * k : a * TILE + 8 * k + 8, :] = source[k, 8 * a : 8 * a + 8, :]
    n = x_ref.shape[0]
    eliminate(x_ref, s_ref, block_ref, parts_ref, 0, n // LANES)
    row = lax.broadcasted_iota(jnp.int32, (n, n), 0)
    column = lax.broadcasted_iota(jnp.int32, (n, n), 1)
    x_ref[...] = jnp.where(column <= row, x_ref[...], 0.0)
    panel_ref[...] = dot(rows_ref[...], x_ref[...], 1, 1)


def panel(top, near):
    pieces, height, n = near.shape
    rows = pieces * height
    return pl.pallas_call(
        panel_kernel,
        out_shape=(jax.ShapeDtypeStruct((rows, n), jnp.float32), jax.ShapeDtypeStruct((n, n), jnp.float32)),
        in_specs=[VMEM, VMEM],
        out_specs=(VMEM, VMEM),
        scratch_shapes=[
            pltpu.VMEM((n, n), jnp.float32),
            pltpu.VMEM((LANES, LANES), jnp.float32),
            pltpu.VMEM((6 * LANES, n), jnp.bfloat16),
            pltpu.VMEM((rows, n), jnp.float32),
        ],
        cost_estimate=pl.CostEstimate(flops=int(8e9), bytes_accessed=3 * 2**20, transcendentals=0),
        compiler_params=pltpu.CompilerParams(vmem_limit_bytes=10 * 2**20),
        name="panel",
    )(top, near)


def schur_kernel(at_ref, parent_ref, panel_ref, x_ref, *refs):
    far_refs = refs[:4]
    out_ref, rows_ref, solved_ref = refs[4:]
    x, zh = at_ref[3], at_ref[4]
    r = pl.program_id(0)

    @pl.when(r == 0)
    def _():
        for dx, far_ref in enumerate(far_refs):
            for dz in range(4):
                k = (x ^ dx) * 4 + (zh ^ dz)
                for a in range(far_ref.shape[1] // 8):
                    rows_ref[pl.ds(pl.multiple_of(a * TILE + 8 * k, 8), 8), :] = far_ref[
                        dz, 8 * a : 8 * a + 8, :
                    ]
        solved_ref[...] = dot(rows_ref[...], x_ref[...], 1, 1)

    step = out_ref.shape[0]
    here = pl.ds(pl.multiple_of(r * step, step), step)
    out_ref[...] = parent_ref[here, :] - split_dot(panel_ref[here, :], solved_ref[...])


def schur(at, parent, panel_rows, inverse, far):
    rows, cols = parent.shape
    n = panel_rows.shape[1]
    step = 256
    return pl.pallas_call(
        schur_kernel,
        grid=(rows // step,),
        out_shape=jax.ShapeDtypeStruct(parent.shape, jnp.float32),
        in_specs=[SMEM] + [VMEM] * 7,
        out_specs=pl.BlockSpec((step, cols), lambda r: (r, 0)),
        scratch_shapes=[pltpu.VMEM((rows, n), jnp.float32), pltpu.VMEM((rows, n), jnp.float32)],
        compiler_params=pltpu.CompilerParams(vmem_limit_bytes=16 * 2**20),
        name="schur",
    )(at, parent, panel_rows, inverse, *far)


def near_kernel(map_ref, at_ref, got_ref, base_ref, out_ref):
    i = at_ref[0]
    offset = got_ref.shape[1] - 16
    out_ref[...] = base_ref[...]
    for s in range(map_ref.shape[0]):
        for c in range(2):
            cb = map_ref[s, c]
            for a in range(2):
                ra = map_ref[s, 2 * i + a]

                @pl.when((ra >= 0) & (cb >= 0) & (cb < PANEL // TILE))
                def _():
                    rows = pl.ds(pl.multiple_of((ra - 8 * i) * 8, 8), 8)
                    lanes = pl.ds(pl.multiple_of(cb * TILE, TILE), TILE)
                    piece = got_ref[2 * s + c, offset + 8 * a : offset + 8 * a + 8, :]
                    out_ref[rows, lanes] = out_ref[rows, lanes] + piece


def assemble_kernel(map_ref, at_ref, got_ref, parent_ref, out_ref):
    i = at_ref[0]
    g = at_ref[1]
    out_ref[...] = parent_ref[...]
    for s in range(map_ref.shape[0]):
        for c in range(2):
            cb = map_ref[s, 2 * g + c]
            for a in range(2):
                ra = map_ref[s, 2 * i + a]

                @pl.when((ra >= 0) & (cb >= 0))
                def _():
                    rows = pl.ds(pl.multiple_of((ra - 8 * i) * TILE, TILE), TILE)
                    lanes = pl.ds(pl.multiple_of((cb - 8 * g) * TILE, TILE), TILE)
                    piece = got_ref[2 * s + c, TILE * a : TILE * a + TILE, :]
                    out_ref[rows, lanes] = out_ref[rows, lanes] + piece


def placed_sum(kernel, name, tile_map, at, got, base):
    return pl.pallas_call(
        kernel,
        out_shape=jax.ShapeDtypeStruct(base.shape, jnp.float32),
        in_specs=[SMEM, SMEM, VMEM, VMEM],
        out_specs=VMEM,
        compiler_params=pltpu.CompilerParams(vmem_limit_bytes=10 * 2**20),
        name=name,
    )(tile_map, at, got, base)


def gathered(value, axis):
    peers = lax.axis_size(axis)
    copies = jnp.broadcast_to(value[None], (peers, *value.shape))
    return lax.all_to_all(copies, axis, 0, 0, tiled=True)


def transposed_pairs():
    pairs = []
    for r in range(16):
        for k in range(16):

            def flat(row, group):
                x, zh = divmod(row, 4)
                y, rest = divmod(group, 4)
                zl, core = divmod(rest, 2)
                return (((y * 2 + zl) * 4 + x) * 4 + zh) * 2 + core

            pairs.append((flat(r, k), flat(k, r)))
    return pairs


def shifted(value, axis, by):
    peers = lax.axis_size(axis)
    return lax.ppermute(value, axis, [(i, (i + by) % peers) for i in range(peers)])


def flipped(value, axis):
    return [value] + [
        lax.ppermute(value, axis, [(i, i ^ by) for i in range(4)]) for by in (1, 2, 3)
    ]


def from_first(value, axis):
    sent = [lax.ppermute(value, axis, [(0, i)]) for i in (1, 2, 3)]
    return jnp.where(lax.axis_index(axis) == 0, value, sent[0] + sent[1] + sent[2])


def rows_to_slices(rows, count):
    total, cols = rows.shape
    tiles = total // (8 * count)
    return rows.reshape(tiles, count, 8, cols).transpose(1, 0, 2, 3).reshape(count, tiles * 8, cols)


def on_device(child_pivot, child_border, child_update, parent_front, tile_map):
    core = lax.axis_index("core")
    row = lax.axis_index(ROW)
    group = lax.axis_index(GRP)
    at = jnp.stack([row, group, core, lax.axis_index("x"), lax.axis_index("zh")]).astype(jnp.int32)
    border = child_border[0]
    n = child_pivot.shape[-1]

    part = lax.dynamic_slice_in_dim(child_pivot[0], core * 32, 32, 0)
    pivot = gathered(part, "zh")
    half = lax.dynamic_slice_in_dim(border, core * TILE, TILE, 0)
    corner = rows_to_slices(parent_front[:, :PANEL], 16).reshape(4, 2, 2, 64, PANEL)
    quarters = [lax.ppermute(corner[q], GRP, [(0, 4 * q)]) for q in (1, 2, 3)]
    corner = jnp.where(lax.axis_index("y") == 0, corner[0], quarters[0] + quarters[1] + quarters[2])
    up = shifted(half, "zh", 1)
    down = shifted(half, "zh", -1)
    pivot, update, corner, up, down = lax.optimization_barrier(
        (pivot, child_update[0], corner, up, down)
    )
    far0 = shifted(up[: TILE // 2], "zh", 1)
    far1 = shifted(down[TILE // 2 :], "zh", -1)
    column = jnp.stack([half, up, down, jnp.concatenate([far0, far1], axis=0)])
    pivot = gathered(pivot, "x")
    keep, send = split_update(at, update)
    sent = lax.ppermute(send, "core", [(0, 1), (1, 0)])
    eighth = lax.ppermute(corner[1], GRP, [(4 * y, 4 * y + 2) for y in range(4)])
    corner = jnp.where(lax.axis_index("zl") == 0, corner[0], eighth)
    pivot, corner, keep, sent, column = lax.optimization_barrier((pivot, corner, keep, sent, column))
    pivot = pivot.reshape(16, 32, n)
    other = lax.ppermute(pivot, "core", [(0, 1), (1, 0)])
    last = lax.ppermute(corner[1], GRP, [(2 * m, 2 * m + 1) for m in range(8)])
    base = jnp.where(core == 0, corner[0], last)

    split = 5
    close, state = elimination(at, pivot, other, n, split)
    up = shifted(column, "x", 1)
    down = shifted(column, "x", -1)
    x_state, s_state, up, down = lax.optimization_barrier((*state, up, down))
    far0 = shifted(up[:2], "x", 1)
    far1 = shifted(down[2:], "x", -1)
    solved = close(x_state, s_state)
    send = contributions(at, solved, border, (column, up, down, far0, far1), keep, sent)
    got = lax.all_to_all(send, GRP, 0, 0, tiled=True)

    mine = placed_sum(near_kernel, "near", tile_map, at, got, base)
    near = gathered(mine, GRP)
    top = from_first(mine[:16], "x")
    top, moved = lax.optimization_barrier((top, mine))
    far = lax.ppermute(moved, AXES, transposed_pairs())
    top = from_first(top, "zh")
    top, far, near = lax.optimization_barrier((top, far, near))
    far = jnp.stack(flipped(far, "zh"))
    top = gathered(top, GRP)
    parent = placed_sum(assemble_kernel, "assemble", tile_map, at, got, parent_front)
    top, near, far, parent = lax.optimization_barrier((top, near, far, parent))
    far = flipped(far, "x")
    panel_rows, inverse = panel(top, near)
    schur_block = schur(at, parent, panel_rows, inverse, far)
    return (schur_block, panel_rows)


def solution(mesh):
    fine = Mesh(mesh.devices.reshape(SIZES), AXES)
    placed = (
        P(SUB, ROW, None),
        P(SUB, ROW, None),
        P(SUB, ROW, "core"),
        P(ROW, GRP),
        P(),
    )
    return jax.shard_map(
        on_device,
        mesh=fine,
        in_specs=placed,
        out_specs=(P(ROW, GRP), P(ROW, None)),
        check_vma=False,
    )
```

```python
import functools

import jax
import jax.numpy as jnp
from jax import lax
from jax.experimental import pallas as pl
from jax.experimental.pallas import tpu as pltpu
from jax.sharding import Mesh, PartitionSpec as P

PANEL = 256
TILE = 128
AXES = ("y", "zl", "x", "zh", "core")
SIZES = (4, 2, 4, 4, 2)
ROW = ("x", "zh")
GRP = ("y", "zl", "core")
SUB = ("y", "zl")
LANES = 128

highest = lax.Precision.HIGHEST
VMEM = pl.BlockSpec(memory_space=pltpu.VMEM)
SMEM = pl.BlockSpec(memory_space=pltpu.SMEM)


def dot(a, b, ca=1, cb=0):
    return lax.dot_general(
        a, b, (((ca,), (cb,)), ((), ())), precision=highest, preferred_element_type=jnp.float32
    )


def halves_of(value):
    high = value.astype(jnp.bfloat16)
    return high, (value - high.astype(jnp.float32)).astype(jnp.bfloat16)


def thirds_of(value):
    high = value.astype(jnp.bfloat16)
    rest = value - high.astype(jnp.float32)
    middle = rest.astype(jnp.bfloat16)
    return high, middle, (rest - middle.astype(jnp.float32)).astype(jnp.bfloat16)


def left_parts(value):
    high, middle, low = thirds_of(value)
    return jnp.concatenate([high, middle, high, middle, high, low], axis=1)


def right_parts(value):
    high, middle, low = thirds_of(value)
    return jnp.concatenate([high, high, middle, middle, low, high], axis=0)


def parts_dot(left, right):
    return lax.dot_general(
        left, right, (((1,), (0,)), ((), ())), preferred_element_type=jnp.float32
    )


def split_dot(a, b):
    a_high, a_low = halves_of(a)
    b_high, b_low = halves_of(b)
    part = lambda p, q: lax.dot_general(
        p, q, (((1,), (1,)), ((), ())), preferred_element_type=jnp.float32
    )
    return part(a_high, b_high) + (part(a_high, b_low) + part(a_low, b_high))


def inverse_factor_rows(groups):
    count = len(groups)
    full = (8, LANES)
    lane = lax.broadcasted_iota(jnp.int32, full, 1)
    sublane = lax.broadcasted_iota(jnp.int32, full, 0)
    d = list(groups)
    out = [None] * count
    for g in range(count):
        base = 8 * g
        inside = (lane >= base) & (lane < base + 8)
        own = d[g]
        cols = [jnp.broadcast_to(own[:, base + q : base + q + 1], full) for q in range(8)]
        e = [[None] * 8 for _ in range(8)]
        for q in range(8):
            for i in range(q, 8):
                e[i][q] = jnp.broadcast_to(cols[q][i : i + 1, :], full)
        y = []
        for i in range(8):
            row = jnp.broadcast_to(own[i : i + 1, :], full)
            y.append(jnp.where(inside, jnp.where(lane == base + i, 1.0, 0.0), row))
        scale = [lax.rsqrt(e[i][i]) for i in range(8)]
        for i in range(8):
            for j in range(i + 1):
                e[i][j] = e[i][j] * scale[i] * scale[j]
            y[i] = y[i] * scale[i]
        inv = [None] * 8
        low = [[None] * 8 for _ in range(8)]
        for p in range(0, 8, 2):
            q = p + 1
            inv[p] = 1.0 / e[p][p]
            inv[q] = e[p][p] / (e[p][p] * e[q][q] - e[q][p] * e[q][p])
            for i in range(q, 8):
                low[i][p] = e[i][p] * inv[p]
                e[i][q] = e[i][q] - low[i][p] * e[q][p]
            y[q] = y[q] - low[q][p] * y[p]
            for i in range(q + 1, 8):
                low[i][q] = e[i][q] * inv[q]
                for j in range(q + 1, i + 1):
                    e[i][j] = e[i][j] - low[i][p] * e[j][p] - low[i][q] * e[j][q]
                y[i] = y[i] - low[i][p] * y[p] - low[i][q] * y[q]
        rows = y[0] * lax.rsqrt(e[0][0])
        for i in range(1, 8):
            rows = jnp.where(sublane == i, y[i] * lax.rsqrt(e[i][i]), rows)
        out[g] = jnp.where(lane <= sublane + base, rows, 0.0)
        if g == count - 1:
            break
        s = [y[i] * inv[i] for i in range(8)]
        for i in range(6, -1, -1):
            for p in range(i + 1, 8):
                s[i] = s[i] - low[p][i] * s[p]
        s = [s[i] * scale[i] for i in range(8)]
        for r in range(g + 1, count):
            acc = jnp.where(inside, 0.0, d[r])
            for q in range(8):
                acc = acc - jnp.broadcast_to(d[r][:, base + q : base + q + 1], full) * s[q]
            d[r] = acc
    return out


def eliminate(x_ref, s_ref, block_ref, parts_ref, first, last):
    n = x_ref.shape[0]
    steps = n // LANES
    square = (LANES, LANES)
    eye = (
        lax.broadcasted_iota(jnp.int32, square, 0) == lax.broadcasted_iota(jnp.int32, square, 1)
    ).astype(jnp.float32)

    def step(k, carry):
        k0 = pl.multiple_of(k * LANES, LANES)
        here = pl.ds(k0, LANES)
        groups = [x_ref[pl.ds(k0 + 8 * r, 8), here] for r in range(LANES // 8)]
        for r, rows in enumerate(inverse_factor_rows(groups)):
            block_ref[8 * r : 8 * r + 8, :] = rows
        x_ref[here, here] = eye
        block = block_ref[...]
        scaled = dot(block, x_ref[here, :])
        solved = dot(block, scaled, 0, 0)
        x_ref[here, :] = scaled
        s_ref[here, :] = solved
        parts_ref[...] = right_parts(solved)

        def update(r, inner):
            there = pl.ds(pl.multiple_of(r * LANES, LANES), LANES)
            below = x_ref[there, here]
            x_ref[there, here] = jnp.zeros(square, jnp.float32)
            x_ref[there, :] = x_ref[there, :] - parts_dot(left_parts(below), parts_ref[...])
            return inner

        lax.fori_loop(k + 1, steps, update, 0)
        return carry

    lax.fori_loop(first, last, step, 0)


def open_kernel(last, at_ref, own_ref, other_ref, x_ref, s_ref, block_ref, parts_ref):
    core = at_ref[2]
    pieces, rows, _ = own_ref.shape
    for i in range(pieces):
        start = i * 2 * rows
        x_ref[pl.ds(pl.multiple_of(start + core * rows, rows), rows), :] = own_ref[i]
        x_ref[pl.ds(pl.multiple_of(start + (1 - core) * rows, rows), rows), :] = other_ref[i]
    eliminate(x_ref, s_ref, block_ref, parts_ref, 0, last)


def close_kernel(first, x_in, s_in, x_ref, s_ref, block_ref, parts_ref):
    del x_in, s_in
    eliminate(x_ref, s_ref, block_ref, parts_ref, first, x_ref.shape[0] // LANES)


def elimination(at, own, other, n, split):
    shape = jax.ShapeDtypeStruct((n, n), jnp.float32)
    common = dict(
        out_shape=(shape, shape),
        out_specs=(VMEM, VMEM),
        scratch_shapes=[
            pltpu.VMEM((LANES, LANES), jnp.float32),
            pltpu.VMEM((6 * LANES, n), jnp.bfloat16),
        ],
        compiler_params=pltpu.CompilerParams(vmem_limit_bytes=10 * 2**20),
    )
    cost = lambda share: pl.CostEstimate(
        flops=int(share * 40e9), bytes_accessed=8 * n * n, transcendentals=0
    )
    state = pl.pallas_call(
        functools.partial(open_kernel, split), in_specs=[SMEM, VMEM, VMEM], cost_estimate=cost(0.66), name="open_factor", **common
    )(at, own, other)
    return lambda x, s: pl.pallas_call(
        functools.partial(close_kernel, split),
        in_specs=[VMEM, VMEM],
        input_output_aliases={0: 0, 1: 1},
        cost_estimate=cost(0.34),
        name="close_factor",
        **common,
    )(x, s)[1], state


def contrib_kernel(offsets, at_ref, s_ref, own_ref, *refs):
    core, x, zh = at_ref[2], at_ref[3], at_ref[4]
    keep_ref, sent_ref, out_ref, w_ref = refs[len(offsets) :]
    depth = s_ref.shape[0]
    rows = own_ref.shape[0]
    w_ref[...] = own_ref[...]

    def step(k, carry):
        here = pl.ds(pl.multiple_of(k * LANES, LANES), LANES)
        pivot = w_ref[:, here]
        w_ref[:, here] = jnp.zeros((rows, LANES), jnp.float32)
        w_ref[...] = w_ref[...] - parts_dot(left_parts(pivot), right_parts(s_ref[here, :]))
        return carry

    lax.fori_loop(0, depth // LANES, step, 0)
    tiles = [(ref, m, at) for ref, ats in zip(refs, offsets) for m, at in enumerate(ats)]
    for first in range(0, len(tiles), 2):
        pair = tiles[first : first + 2]
        block = jnp.concatenate([ref[m] for ref, m, _ in pair], axis=0)
        product = dot(w_ref[...], block, 1, 1)
        for t, (_, _, (dx, dz)) in enumerate(pair):
            j = ((x + dx) & 3) * 4 + ((zh + dz) & 3)
            mine = (j // 8) == core
            inner = j % 8
            u = jnp.where(mine, keep_ref[inner], sent_ref[inner])
            out_ref[j, 0:rows, :] = u + product[:, t * TILE : (t + 1) * TILE]
    for k in range(16):
        for a in range(2):
            out_ref[k, rows + 8 * a : rows + 8 * a + 8, :] = out_ref[
                0, a * TILE + 8 * k : a * TILE + 8 * k + 8, :
            ]


def contributions(at, solved, border, pieces, offsets, keep, sent):
    rows = border.shape[0]
    return pl.pallas_call(
        functools.partial(contrib_kernel, offsets),
        out_shape=jax.ShapeDtypeStruct((16, rows + 16, TILE), jnp.float32),
        in_specs=[SMEM] + [VMEM] * (4 + len(pieces)),
        out_specs=VMEM,
        scratch_shapes=[pltpu.VMEM(border.shape, jnp.float32)],
        compiler_params=pltpu.CompilerParams(vmem_limit_bytes=10 * 2**20),
        name="contributions",
    )(at, solved, border, *pieces, keep, sent)


def split_kernel(at_ref, u_ref, keep_ref, send_ref):
    core = at_ref[2]
    for m in range(keep_ref.shape[0]):
        keep_ref[m] = u_ref[:, pl.ds(pl.multiple_of((2 * m + core) * TILE, TILE), TILE)]
        send_ref[m] = u_ref[:, pl.ds(pl.multiple_of((2 * m + 1 - core) * TILE, TILE), TILE)]


def split_update(at, update):
    rows, cols = update.shape
    shape = jax.ShapeDtypeStruct((cols // (2 * TILE), rows, TILE), jnp.float32)
    return pl.pallas_call(
        split_kernel,
        out_shape=(shape, shape),
        in_specs=[SMEM, VMEM],
        out_specs=(VMEM, VMEM),
        name="split_update",
    )(at, update)


def panel_kernel(both_ref, panel_ref, x_ref, s_ref, block_ref, parts_ref, rows_ref):
    near = rows_ref.shape[0] // TILE
    for k in range(both_ref.shape[0]):
        for a in range(both_ref.shape[1] // 8):
            to, at = (rows_ref, a) if a < near else (x_ref, a - near)
            to[at * TILE + 8 * k : at * TILE + 8 * k + 8, :] = both_ref[k, 8 * a : 8 * a + 8, :]
    n = x_ref.shape[0]
    eliminate(x_ref, s_ref, block_ref, parts_ref, 0, n // LANES)
    row = lax.broadcasted_iota(jnp.int32, (n, n), 0)
    column = lax.broadcasted_iota(jnp.int32, (n, n), 1)
    x_ref[...] = jnp.where(column <= row, x_ref[...], 0.0)
    panel_ref[...] = dot(rows_ref[...], x_ref[...], 1, 1)


def panel(both):
    pieces, height, n = both.shape
    rows = pieces * height - n
    return pl.pallas_call(
        panel_kernel,
        out_shape=(jax.ShapeDtypeStruct((rows, n), jnp.float32), jax.ShapeDtypeStruct((n, n), jnp.float32)),
        in_specs=[VMEM],
        out_specs=(VMEM, VMEM),
        scratch_shapes=[
            pltpu.VMEM((n, n), jnp.float32),
            pltpu.VMEM((LANES, LANES), jnp.float32),
            pltpu.VMEM((6 * LANES, n), jnp.bfloat16),
            pltpu.VMEM((rows, n), jnp.float32),
        ],
        cost_estimate=pl.CostEstimate(flops=int(8e9), bytes_accessed=3 * 2**20, transcendentals=0),
        compiler_params=pltpu.CompilerParams(vmem_limit_bytes=10 * 2**20),
        name="panel",
    )(both)


def schur_kernel(at_ref, parent_ref, panel_ref, x_ref, *refs):
    far_refs = refs[:4]
    out_ref, rows_ref, solved_ref = refs[4:]
    x, zh = at_ref[3], at_ref[4]
    r = pl.program_id(0)

    @pl.when(r == 0)
    def _():
        for dx, far_ref in enumerate(far_refs):
            for dz in range(4):
                k = (x ^ dx) * 4 + (zh ^ dz)
                for a in range(far_ref.shape[1] // 8):
                    rows_ref[pl.ds(pl.multiple_of(a * TILE + 8 * k, 8), 8), :] = far_ref[
                        dz, 8 * a : 8 * a + 8, :
                    ]
        solved_ref[...] = dot(rows_ref[...], x_ref[...], 1, 1)

    step = out_ref.shape[0]
    here = pl.ds(pl.multiple_of(r * step, step), step)
    out_ref[...] = parent_ref[here, :] - split_dot(panel_ref[here, :], solved_ref[...])


def schur(at, parent, panel_rows, inverse, far):
    rows, cols = parent.shape
    n = panel_rows.shape[1]
    step = 256
    return pl.pallas_call(
        schur_kernel,
        grid=(rows // step,),
        out_shape=jax.ShapeDtypeStruct(parent.shape, jnp.float32),
        in_specs=[SMEM] + [VMEM] * 7,
        out_specs=pl.BlockSpec((step, cols), lambda r: (r, 0)),
        scratch_shapes=[pltpu.VMEM((rows, n), jnp.float32), pltpu.VMEM((rows, n), jnp.float32)],
        compiler_params=pltpu.CompilerParams(vmem_limit_bytes=16 * 2**20),
        name="schur",
    )(at, parent, panel_rows, inverse, *far)


def near_kernel(map_ref, at_ref, got_ref, base_ref, out_ref):
    i = at_ref[0]
    offset = got_ref.shape[1] - 16
    out_ref[...] = base_ref[...]
    for s in range(map_ref.shape[0]):
        for c in range(2):
            cb = map_ref[s, c]
            for a in range(2):
                ra = map_ref[s, 2 * i + a]

                @pl.when((ra >= 0) & (cb >= 0) & (cb < PANEL // TILE))
                def _():
                    rows = pl.ds(pl.multiple_of((ra - 8 * i) * 8, 8), 8)
                    lanes = pl.ds(pl.multiple_of(cb * TILE, TILE), TILE)
                    piece = got_ref[2 * s + c, offset + 8 * a : offset + 8 * a + 8, :]
                    out_ref[rows, lanes] = out_ref[rows, lanes] + piece


def assemble_kernel(map_ref, at_ref, got_ref, parent_ref, out_ref):
    i = at_ref[0]
    g = at_ref[1]
    out_ref[...] = parent_ref[...]
    for s in range(map_ref.shape[0]):
        for c in range(2):
            cb = map_ref[s, 2 * g + c]
            for a in range(2):
                ra = map_ref[s, 2 * i + a]

                @pl.when((ra >= 0) & (cb >= 0))
                def _():
                    rows = pl.ds(pl.multiple_of((ra - 8 * i) * TILE, TILE), TILE)
                    lanes = pl.ds(pl.multiple_of((cb - 8 * g) * TILE, TILE), TILE)
                    piece = got_ref[2 * s + c, TILE * a : TILE * a + TILE, :]
                    out_ref[rows, lanes] = out_ref[rows, lanes] + piece


def placed_sum(kernel, name, tile_map, at, got, base):
    return pl.pallas_call(
        kernel,
        out_shape=jax.ShapeDtypeStruct(base.shape, jnp.float32),
        in_specs=[SMEM, SMEM, VMEM, VMEM],
        out_specs=VMEM,
        compiler_params=pltpu.CompilerParams(vmem_limit_bytes=10 * 2**20),
        name=name,
    )(tile_map, at, got, base)


def gathered(value, axis):
    peers = lax.axis_size(axis)
    copies = jnp.broadcast_to(value[None], (peers, *value.shape))
    return lax.all_to_all(copies, axis, 0, 0, tiled=True)


def transposed_pairs():
    pairs = []
    for r in range(16):
        for k in range(16):

            def flat(row, group):
                x, zh = divmod(row, 4)
                y, rest = divmod(group, 4)
                zl, core = divmod(rest, 2)
                return (((y * 2 + zl) * 4 + x) * 4 + zh) * 2 + core

            pairs.append((flat(r, k), flat(k, r)))
    return pairs


def shifted(value, axis, by):
    peers = lax.axis_size(axis)
    return lax.ppermute(value, axis, [(i, (i + by) % peers) for i in range(peers)])


def flipped(value, axis):
    return [value] + [
        lax.ppermute(value, axis, [(i, i ^ by) for i in range(4)]) for by in (1, 2, 3)
    ]


def rows_to_slices(rows, count):
    total, cols = rows.shape
    tiles = total // (8 * count)
    return rows.reshape(tiles, count, 8, cols).transpose(1, 0, 2, 3).reshape(count, tiles * 8, cols)


def on_device(child_pivot, child_border, child_update, parent_front, tile_map):
    core = lax.axis_index("core")
    row = lax.axis_index(ROW)
    group = lax.axis_index(GRP)
    at = jnp.stack([row, group, core, lax.axis_index("x"), lax.axis_index("zh")]).astype(jnp.int32)
    border = child_border[0]
    n = child_pivot.shape[-1]

    part = lax.dynamic_slice_in_dim(child_pivot[0], core * 32, 32, 0)
    pivot = gathered(part, "zh")
    half = lax.dynamic_slice_in_dim(border, core * TILE, TILE, 0)
    corner = rows_to_slices(parent_front[:, :PANEL], 16).reshape(4, 2, 2, 64, PANEL)
    quarters = [lax.ppermute(corner[q], GRP, [(0, 4 * q)]) for q in (1, 2, 3)]
    corner = jnp.where(lax.axis_index("y") == 0, corner[0], quarters[0] + quarters[1] + quarters[2])
    pivot, half, update, corner = lax.optimization_barrier((pivot, half, child_update[0], corner))
    up = shifted(half, "zh", 1)
    down = shifted(half, "zh", -1)
    most = jnp.stack([half, up, down])
    far0 = shifted(up[: TILE // 2], "zh", 1)
    far1 = shifted(down[TILE // 2 :], "zh", -1)
    most_up = shifted(most, "x", 1)
    most_down = shifted(most, "x", -1)
    rest = jnp.concatenate([far0, far1], axis=0)[None]
    pivot = gathered(pivot, "x")
    keep, send = split_update(at, update)
    sent = lax.ppermute(send, "core", [(0, 1), (1, 0)])
    eighth = lax.ppermute(corner[1], GRP, [(4 * y, 4 * y + 2) for y in range(4)])
    corner = jnp.where(lax.axis_index("zl") == 0, corner[0], eighth)
    pivot, corner, keep, sent, rest = lax.optimization_barrier((pivot, corner, keep, sent, rest))
    pivot = pivot.reshape(16, 32, n)
    other = lax.ppermute(pivot, "core", [(0, 1), (1, 0)])
    last = lax.ppermute(corner[1], GRP, [(2 * m, 2 * m + 1) for m in range(8)])
    base = jnp.where(core == 0, corner[0], last)
    rest_up = shifted(rest, "x", 1)
    rest_down = shifted(rest, "x", -1)

    split = 5
    close, state = elimination(at, pivot, other, n, split)
    x_state, s_state, most_up, most_down, rest_up, rest_down = lax.optimization_barrier(
        (*state, most_up, most_down, rest_up, rest_down)
    )
    over0 = shifted(most_up[:2], "x", 1)
    over1 = shifted(most_down[2:], "x", -1)
    over2 = shifted(rest_down, "x", -1)
    solved = close(x_state, s_state)
    pieces = (most, most_up, most_down, over0, over1, rest, rest_up, rest_down, over2)
    near_zh, far_zh = (0, -1, 1), (2,)
    offsets = tuple(
        tuple((dx, dz) for dz in dzs)
        for dx, dzs in (
            (0, near_zh),
            (-1, near_zh),
            (1, near_zh),
            (2, near_zh[:2]),
            (2, near_zh[2:]),
            (0, far_zh),
            (-1, far_zh),
            (1, far_zh),
            (2, far_zh),
        )
    )
    send = contributions(at, solved, border, pieces, offsets, keep, sent)
    got = lax.all_to_all(send, GRP, 0, 0, tiled=True)

    mine = placed_sum(near_kernel, "near", tile_map, at, got, base)
    top = gathered(gathered(mine[:16], "x")[0], "zh")[0]
    both = gathered(jnp.concatenate([mine, top], axis=0), GRP)
    top, moved = lax.optimization_barrier((top, mine))
    far = lax.ppermute(moved, AXES, transposed_pairs())
    far = jnp.stack(flipped(far, "zh"))
    parent = placed_sum(assemble_kernel, "assemble", tile_map, at, got, parent_front)
    both, far, parent = lax.optimization_barrier((both, far, parent))
    far = flipped(far, "x")
    panel_rows, inverse = panel(both)
    schur_block = schur(at, parent, panel_rows, inverse, far)
    return (schur_block, panel_rows)


def solution(mesh):
    fine = Mesh(mesh.devices.reshape(SIZES), AXES)
    placed = (
        P(SUB, ROW, None),
        P(SUB, ROW, None),
        P(SUB, ROW, "core"),
        P(ROW, GRP),
        P(),
    )
    return jax.shard_map(
        on_device,
        mesh=fine,
        in_specs=placed,
        out_specs=(P(ROW, GRP), P(ROW, None)),
        check_vma=False,
    )
```

```python
import functools

import jax
import jax.numpy as jnp
from jax import lax
from jax.experimental import pallas as pl
from jax.experimental.pallas import tpu as pltpu
from jax.sharding import Mesh, PartitionSpec as P

PANEL = 256
TILE = 128
AXES = ("y", "zl", "x", "zh", "core")
SIZES = (4, 2, 4, 4, 2)
ROW = ("x", "zh")
GRP = ("y", "zl", "core")
SUB = ("y", "zl")
LANES = 128

highest = lax.Precision.HIGHEST
VMEM = pl.BlockSpec(memory_space=pltpu.VMEM)
SMEM = pl.BlockSpec(memory_space=pltpu.SMEM)


def dot(a, b, ca=1, cb=0):
    return lax.dot_general(
        a, b, (((ca,), (cb,)), ((), ())), precision=highest, preferred_element_type=jnp.float32
    )


def halves_of(value):
    high = value.astype(jnp.bfloat16)
    return high, (value - high.astype(jnp.float32)).astype(jnp.bfloat16)


def thirds_of(value):
    high = value.astype(jnp.bfloat16)
    rest = value - high.astype(jnp.float32)
    middle = rest.astype(jnp.bfloat16)
    return high, middle, (rest - middle.astype(jnp.float32)).astype(jnp.bfloat16)


def left_parts(value):
    high, middle, low = thirds_of(value)
    return jnp.concatenate([high, middle, high, middle, high, low], axis=1)


def right_parts(value):
    high, middle, low = thirds_of(value)
    return jnp.concatenate([high, high, middle, middle, low, high], axis=0)


def parts_dot(left, right):
    return lax.dot_general(
        left, right, (((1,), (0,)), ((), ())), preferred_element_type=jnp.float32
    )


def split_dot(a, b):
    a_high, a_low = halves_of(a)
    b_high, b_low = halves_of(b)
    part = lambda p, q: lax.dot_general(
        p, q, (((1,), (1,)), ((), ())), preferred_element_type=jnp.float32
    )
    return part(a_high, b_high) + (part(a_high, b_low) + part(a_low, b_high))


def inverse_factor_rows(groups):
    count = len(groups)
    full = (8, LANES)
    lane = lax.broadcasted_iota(jnp.int32, full, 1)
    sublane = lax.broadcasted_iota(jnp.int32, full, 0)
    d = list(groups)
    out = [None] * count
    for g in range(count):
        base = 8 * g
        inside = (lane >= base) & (lane < base + 8)
        own = d[g]
        cols = [jnp.broadcast_to(own[:, base + q : base + q + 1], full) for q in range(8)]
        e = [[None] * 8 for _ in range(8)]
        for q in range(8):
            for i in range(q, 8):
                e[i][q] = jnp.broadcast_to(cols[q][i : i + 1, :], full)
        y = []
        for i in range(8):
            row = jnp.broadcast_to(own[i : i + 1, :], full)
            y.append(jnp.where(inside, jnp.where(lane == base + i, 1.0, 0.0), row))
        scale = [lax.rsqrt(e[i][i]) for i in range(8)]
        for i in range(8):
            for j in range(i + 1):
                e[i][j] = e[i][j] * scale[i] * scale[j]
            y[i] = y[i] * scale[i]
        inv = [None] * 8
        low = [[None] * 8 for _ in range(8)]
        for p in range(0, 8, 2):
            q = p + 1
            inv[p] = 1.0 / e[p][p]
            inv[q] = e[p][p] / (e[p][p] * e[q][q] - e[q][p] * e[q][p])
            for i in range(q, 8):
                low[i][p] = e[i][p] * inv[p]
                e[i][q] = e[i][q] - low[i][p] * e[q][p]
            y[q] = y[q] - low[q][p] * y[p]
            for i in range(q + 1, 8):
                low[i][q] = e[i][q] * inv[q]
                for j in range(q + 1, i + 1):
                    e[i][j] = e[i][j] - low[i][p] * e[j][p] - low[i][q] * e[j][q]
                y[i] = y[i] - low[i][p] * y[p] - low[i][q] * y[q]
        rows = y[0] * lax.rsqrt(e[0][0])
        for i in range(1, 8):
            rows = jnp.where(sublane == i, y[i] * lax.rsqrt(e[i][i]), rows)
        out[g] = jnp.where(lane <= sublane + base, rows, 0.0)
        if g == count - 1:
            break
        s = [y[i] * inv[i] for i in range(8)]
        for i in range(6, -1, -1):
            for p in range(i + 1, 8):
                s[i] = s[i] - low[p][i] * s[p]
        s = [s[i] * scale[i] for i in range(8)]
        for r in range(g + 1, count):
            acc = jnp.where(inside, 0.0, d[r])
            for q in range(8):
                acc = acc - jnp.broadcast_to(d[r][:, base + q : base + q + 1], full) * s[q]
            d[r] = acc
    return out


def eliminate(x_ref, s_ref, block_ref, parts_ref, first, last):
    n = x_ref.shape[0]
    steps = n // LANES
    square = (LANES, LANES)
    eye = (
        lax.broadcasted_iota(jnp.int32, square, 0) == lax.broadcasted_iota(jnp.int32, square, 1)
    ).astype(jnp.float32)

    def step(k, carry):
        k0 = pl.multiple_of(k * LANES, LANES)
        here = pl.ds(k0, LANES)
        groups = [x_ref[pl.ds(k0 + 8 * r, 8), here] for r in range(LANES // 8)]
        for r, rows in enumerate(inverse_factor_rows(groups)):
            block_ref[8 * r : 8 * r + 8, :] = rows
        x_ref[here, here] = eye
        block = block_ref[...]
        parts_ref[...] = right_parts(x_ref[here, :])
        scaled = parts_dot(left_parts(block), parts_ref[...])
        parts_ref[...] = right_parts(scaled)
        solved = parts_dot(left_parts(block.T), parts_ref[...])
        x_ref[here, :] = scaled
        s_ref[here, :] = solved
        parts_ref[...] = right_parts(solved)

        def update(r, inner):
            there = pl.ds(pl.multiple_of(r * LANES, LANES), LANES)
            below = x_ref[there, here]
            x_ref[there, here] = jnp.zeros(square, jnp.float32)
            x_ref[there, :] = x_ref[there, :] - parts_dot(left_parts(below), parts_ref[...])
            return inner

        lax.fori_loop(k + 1, steps, update, 0)
        return carry

    lax.fori_loop(first, last, step, 0)


def open_kernel(last, at_ref, own_ref, other_ref, x_ref, s_ref, block_ref, parts_ref):
    core = at_ref[2]
    pieces, rows, _ = own_ref.shape
    for i in range(pieces):
        start = i * 2 * rows
        x_ref[pl.ds(pl.multiple_of(start + core * rows, rows), rows), :] = own_ref[i]
        x_ref[pl.ds(pl.multiple_of(start + (1 - core) * rows, rows), rows), :] = other_ref[i]
    eliminate(x_ref, s_ref, block_ref, parts_ref, 0, last)


def close_kernel(first, x_in, s_in, x_ref, s_ref, block_ref, parts_ref):
    del x_in, s_in
    eliminate(x_ref, s_ref, block_ref, parts_ref, first, x_ref.shape[0] // LANES)


def elimination(at, own, other, n, split):
    shape = jax.ShapeDtypeStruct((n, n), jnp.float32)
    common = dict(
        out_shape=(shape, shape),
        out_specs=(VMEM, VMEM),
        scratch_shapes=[
            pltpu.VMEM((LANES, LANES), jnp.float32),
            pltpu.VMEM((6 * LANES, n), jnp.bfloat16),
        ],
        compiler_params=pltpu.CompilerParams(vmem_limit_bytes=10 * 2**20),
    )
    cost = lambda share: pl.CostEstimate(
        flops=int(share * 40e9), bytes_accessed=8 * n * n, transcendentals=0
    )
    state = pl.pallas_call(
        functools.partial(open_kernel, split), in_specs=[SMEM, VMEM, VMEM], cost_estimate=cost(0.66), name="open_factor", **common
    )(at, own, other)
    return lambda x, s: pl.pallas_call(
        functools.partial(close_kernel, split),
        in_specs=[VMEM, VMEM],
        input_output_aliases={0: 0, 1: 1},
        cost_estimate=cost(0.34),
        name="close_factor",
        **common,
    )(x, s)[1], state


def contrib_kernel(pieces, at_ref, s_ref, own_ref, *refs):
    core, x, zh = at_ref[2], at_ref[3], at_ref[4]
    keep_ref, sent_ref, out_ref, w_ref = refs[len(pieces) :]
    depth = s_ref.shape[0]
    rows = own_ref.shape[0]
    w_ref[...] = own_ref[...]

    def step(k, carry):
        here = pl.ds(pl.multiple_of(k * LANES, LANES), LANES)
        pivot = w_ref[:, here]
        w_ref[:, here] = jnp.zeros((rows, LANES), jnp.float32)
        w_ref[...] = w_ref[...] - parts_dot(left_parts(pivot), right_parts(s_ref[here, :]))
        return carry

    lax.fori_loop(0, depth // LANES, step, 0)
    for ref, (dx, first, pairs) in zip(refs, pieces):

        def pair(m, carry, ref=ref, dx=dx, first=first):
            block = ref[pl.ds(2 * m, 2)].reshape(2 * TILE, depth)
            product = dot(w_ref[...], block, 1, 1)
            where = first + m
            for t, dz in enumerate((where, 3 * where - 1)):
                j = ((x + dx) & 3) * 4 + ((zh + dz) & 3)
                mine = (j // 8) == core
                inner = j % 8
                u = jnp.where(mine, keep_ref[inner], sent_ref[inner])
                out_ref[j, 0:rows, :] = u + product[:, t * TILE : (t + 1) * TILE]
            return carry

        lax.fori_loop(0, pairs, pair, 0)
    for k in range(16):
        for a in range(2):
            out_ref[k, rows + 8 * a : rows + 8 * a + 8, :] = out_ref[
                0, a * TILE + 8 * k : a * TILE + 8 * k + 8, :
            ]


PIECES = ((0, 0, 2), (-1, 0, 2), (1, 0, 2), (2, 0, 1), (2, 1, 1))


def contributions(at, solved, border, pieces, keep, sent):
    rows = border.shape[0]
    return pl.pallas_call(
        functools.partial(contrib_kernel, PIECES),
        out_shape=jax.ShapeDtypeStruct((16, rows + 16, TILE), jnp.float32),
        in_specs=[SMEM] + [VMEM] * (4 + len(pieces)),
        out_specs=VMEM,
        scratch_shapes=[pltpu.VMEM(border.shape, jnp.float32)],
        compiler_params=pltpu.CompilerParams(vmem_limit_bytes=10 * 2**20),
        name="contributions",
    )(at, solved, border, *pieces, keep, sent)


def split_kernel(at_ref, u_ref, keep_ref, send_ref):
    core = at_ref[2]
    for m in range(keep_ref.shape[0]):
        keep_ref[m] = u_ref[:, pl.ds(pl.multiple_of((2 * m + core) * TILE, TILE), TILE)]
        send_ref[m] = u_ref[:, pl.ds(pl.multiple_of((2 * m + 1 - core) * TILE, TILE), TILE)]


def split_update(at, update):
    rows, cols = update.shape
    shape = jax.ShapeDtypeStruct((cols // (2 * TILE), rows, TILE), jnp.float32)
    return pl.pallas_call(
        split_kernel,
        out_shape=(shape, shape),
        in_specs=[SMEM, VMEM],
        out_specs=(VMEM, VMEM),
        name="split_update",
    )(at, update)


def rows_dot(out_ref, rows_ref, x_ref):
    step = 256

    def chunk(m, carry):
        here = pl.ds(pl.multiple_of(m * step, step), step)
        out_ref[here, :] = dot(rows_ref[here, :], x_ref[...], 1, 1)
        return carry

    lax.fori_loop(0, out_ref.shape[0] // step, chunk, 0)


def panel_kernel(both_ref, panel_ref, x_ref, s_ref, block_ref, parts_ref, rows_ref):
    near = rows_ref.shape[0] // TILE
    for k in range(both_ref.shape[0]):
        for a in range(both_ref.shape[1] // 8):
            to, at = (rows_ref, a) if a < near else (x_ref, a - near)
            to[at * TILE + 8 * k : at * TILE + 8 * k + 8, :] = both_ref[k, 8 * a : 8 * a + 8, :]
    n = x_ref.shape[0]
    eliminate(x_ref, s_ref, block_ref, parts_ref, 0, n // LANES)
    row = lax.broadcasted_iota(jnp.int32, (n, n), 0)
    column = lax.broadcasted_iota(jnp.int32, (n, n), 1)
    x_ref[...] = jnp.where(column <= row, x_ref[...], 0.0)
    rows_dot(panel_ref, rows_ref, x_ref)


def panel(both):
    pieces, height, n = both.shape
    rows = pieces * height - n
    return pl.pallas_call(
        panel_kernel,
        out_shape=(jax.ShapeDtypeStruct((rows, n), jnp.float32), jax.ShapeDtypeStruct((n, n), jnp.float32)),
        in_specs=[VMEM],
        out_specs=(VMEM, VMEM),
        scratch_shapes=[
            pltpu.VMEM((n, n), jnp.float32),
            pltpu.VMEM((LANES, LANES), jnp.float32),
            pltpu.VMEM((6 * LANES, n), jnp.bfloat16),
            pltpu.VMEM((rows, n), jnp.float32),
        ],
        cost_estimate=pl.CostEstimate(flops=int(8e9), bytes_accessed=3 * 2**20, transcendentals=0),
        compiler_params=pltpu.CompilerParams(vmem_limit_bytes=10 * 2**20),
        name="panel",
    )(both)


def schur_kernel(at_ref, parent_ref, panel_ref, x_ref, *refs):
    far_refs = refs[:4]
    out_ref, rows_ref, solved_ref = refs[4:]
    x, zh = at_ref[3], at_ref[4]
    r = pl.program_id(0)

    @pl.when(r == 0)
    def _():
        for dx, far_ref in enumerate(far_refs):
            for dz in range(4):
                k = (x ^ dx) * 4 + (zh ^ dz)
                for a in range(far_ref.shape[1] // 8):
                    rows_ref[pl.ds(pl.multiple_of(a * TILE + 8 * k, 8), 8), :] = far_ref[
                        dz, 8 * a : 8 * a + 8, :
                    ]
        rows_dot(solved_ref, rows_ref, x_ref)

    step = out_ref.shape[0]
    here = pl.ds(pl.multiple_of(r * step, step), step)
    out_ref[...] = parent_ref[here, :] - split_dot(panel_ref[here, :], solved_ref[...])


def schur(at, parent, panel_rows, inverse, far):
    rows, cols = parent.shape
    n = panel_rows.shape[1]
    step = 256
    return pl.pallas_call(
        schur_kernel,
        grid=(rows // step,),
        out_shape=jax.ShapeDtypeStruct(parent.shape, jnp.float32),
        in_specs=[SMEM] + [VMEM] * 7,
        out_specs=pl.BlockSpec((step, cols), lambda r: (r, 0)),
        scratch_shapes=[pltpu.VMEM((rows, n), jnp.float32), pltpu.VMEM((rows, n), jnp.float32)],
        compiler_params=pltpu.CompilerParams(vmem_limit_bytes=16 * 2**20),
        name="schur",
    )(at, parent, panel_rows, inverse, *far)


def near_kernel(map_ref, at_ref, got_ref, base_ref, out_ref):
    i = at_ref[0]
    offset = got_ref.shape[1] - 16
    out_ref[...] = base_ref[...]

    def child(s, carry):
        for c in range(2):
            cb = map_ref[s, c]
            for a in range(2):
                ra = map_ref[s, 2 * i + a]

                @pl.when((ra >= 0) & (cb >= 0) & (cb < PANEL // TILE))
                def _():
                    rows = pl.ds(pl.multiple_of((ra - 8 * i) * 8, 8), 8)
                    lanes = pl.ds(pl.multiple_of(cb * TILE, TILE), TILE)
                    piece = got_ref[2 * s + c, offset + 8 * a : offset + 8 * a + 8, :]
                    out_ref[rows, lanes] = out_ref[rows, lanes] + piece

        return carry

    lax.fori_loop(0, map_ref.shape[0], child, 0)


def assemble_kernel(map_ref, at_ref, got_ref, parent_ref, out_ref):
    i = at_ref[0]
    g = at_ref[1]
    out_ref[...] = parent_ref[...]

    def child(s, carry):
        for c in range(2):
            cb = map_ref[s, 2 * g + c]
            for a in range(2):
                ra = map_ref[s, 2 * i + a]

                @pl.when((ra >= 0) & (cb >= 0))
                def _():
                    rows = pl.ds(pl.multiple_of((ra - 8 * i) * TILE, TILE), TILE)
                    lanes = pl.ds(pl.multiple_of((cb - 8 * g) * TILE, TILE), TILE)
                    piece = got_ref[2 * s + c, TILE * a : TILE * a + TILE, :]
                    out_ref[rows, lanes] = out_ref[rows, lanes] + piece

        return carry

    lax.fori_loop(0, map_ref.shape[0], child, 0)


def placed_sum(kernel, name, tile_map, at, got, base):
    return pl.pallas_call(
        kernel,
        out_shape=jax.ShapeDtypeStruct(base.shape, jnp.float32),
        in_specs=[SMEM, SMEM, VMEM, VMEM],
        out_specs=VMEM,
        compiler_params=pltpu.CompilerParams(vmem_limit_bytes=10 * 2**20),
        name=name,
    )(tile_map, at, got, base)


def gathered(value, axis):
    peers = lax.axis_size(axis)
    copies = jnp.broadcast_to(value[None], (peers, *value.shape))
    return lax.all_to_all(copies, axis, 0, 0, tiled=True)


def transposed_pairs():
    pairs = []
    for r in range(16):
        for k in range(16):

            def flat(row, group):
                x, zh = divmod(row, 4)
                y, rest = divmod(group, 4)
                zl, core = divmod(rest, 2)
                return (((y * 2 + zl) * 4 + x) * 4 + zh) * 2 + core

            pairs.append((flat(r, k), flat(k, r)))
    return pairs


def shifted(value, axis, by):
    peers = lax.axis_size(axis)
    return lax.ppermute(value, axis, [(i, (i + by) % peers) for i in range(peers)])


def ring_pieces(value, axis):
    middle = value.shape[0] // 2
    up = shifted(value, axis, 1)
    down = shifted(value, axis, -1)
    return up, down, shifted(up[:middle], axis, 1), shifted(down[middle:], axis, -1)


def flipped(value, axis):
    return [value] + [
        lax.ppermute(value, axis, [(i, i ^ by) for i in range(4)]) for by in (1, 2, 3)
    ]


def rows_to_slices(rows, count):
    total, cols = rows.shape
    tiles = total // (8 * count)
    return rows.reshape(tiles, count, 8, cols).transpose(1, 0, 2, 3).reshape(count, tiles * 8, cols)


def on_device(child_pivot, child_border, child_update, parent_front, tile_map):
    core = lax.axis_index("core")
    row = lax.axis_index(ROW)
    group = lax.axis_index(GRP)
    at = jnp.stack([row, group, core, lax.axis_index("x"), lax.axis_index("zh")]).astype(jnp.int32)
    border = child_border[0]
    n = child_pivot.shape[-1]

    part = lax.dynamic_slice_in_dim(child_pivot[0], core * 32, 32, 0)
    pivot = gathered(part, "zh")
    half = lax.dynamic_slice_in_dim(border, core * TILE, TILE, 0)
    corner = rows_to_slices(parent_front[:, :PANEL], 16).reshape(4, 2, 2, 64, PANEL)
    quarters = [lax.ppermute(corner[q], GRP, [(0, 4 * q)]) for q in (1, 2, 3)]
    corner = jnp.where(lax.axis_index("y") == 0, corner[0], quarters[0] + quarters[1] + quarters[2])
    pivot, half, update, corner = lax.optimization_barrier((pivot, half, child_update[0], corner))
    up, down, far0, far1 = ring_pieces(half, "zh")
    column = jnp.stack([half, up, down, jnp.concatenate([far0, far1], axis=0)])
    pivot = gathered(pivot, "x")
    keep, send = split_update(at, update)
    sent = lax.ppermute(send, "core", [(0, 1), (1, 0)])
    eighth = lax.ppermute(corner[1], GRP, [(4 * y, 4 * y + 2) for y in range(4)])
    corner = jnp.where(lax.axis_index("zl") == 0, corner[0], eighth)
    pivot, corner, keep, sent, column = lax.optimization_barrier((pivot, corner, keep, sent, column))
    pivot = pivot.reshape(16, 32, n)
    other = lax.ppermute(pivot, "core", [(0, 1), (1, 0)])
    last = lax.ppermute(corner[1], GRP, [(2 * m, 2 * m + 1) for m in range(8)])
    base = jnp.where(core == 0, corner[0], last)

    split = 5
    close, state = elimination(at, pivot, other, n, split)
    up = shifted(column, "x", 1)
    down = shifted(column, "x", -1)
    x_state, s_state, up, down = lax.optimization_barrier((*state, up, down))
    far0 = shifted(up[:2], "x", 1)
    far1 = shifted(down[2:], "x", -1)
    solved = close(x_state, s_state)
    send = contributions(at, solved, border, (column, up, down, far0, far1), keep, sent)
    got = lax.all_to_all(send, GRP, 0, 0, tiled=True)

    mine = placed_sum(near_kernel, "near", tile_map, at, got, base)
    top = gathered(gathered(mine[:16], "x")[0], "zh")[0]
    both = gathered(jnp.concatenate([mine, top], axis=0), GRP)
    top, moved = lax.optimization_barrier((top, mine))
    far = lax.ppermute(moved, AXES, transposed_pairs())
    far = jnp.stack(flipped(far, "zh"))
    parent = placed_sum(assemble_kernel, "assemble", tile_map, at, got, parent_front)
    both, far, parent = lax.optimization_barrier((both, far, parent))
    far = flipped(far, "x")
    panel_rows, inverse = panel(both)
    schur_block = schur(at, parent, panel_rows, inverse, far)
    return (schur_block, panel_rows)


def solution(mesh):
    fine = Mesh(mesh.devices.reshape(SIZES), AXES)
    placed = (
        P(SUB, ROW, None),
        P(SUB, ROW, None),
        P(SUB, ROW, "core"),
        P(ROW, GRP),
        P(),
    )
    return jax.shard_map(
        on_device,
        mesh=fine,
        in_specs=placed,
        out_specs=(P(ROW, GRP), P(ROW, None)),
        check_vma=False,
    )
```

```python
import functools

import jax
import jax.numpy as jnp
from jax import lax
from jax.experimental import pallas as pl
from jax.experimental.pallas import tpu as pltpu
from jax.sharding import Mesh, PartitionSpec as P

PANEL = 256
TILE = 128
AXES = ("y", "zl", "x", "zh", "core")
SIZES = (4, 2, 4, 4, 2)
ROW = ("x", "zh")
GRP = ("y", "zl", "core")
SUB = ("y", "zl")
LANES = 128

highest = lax.Precision.HIGHEST
VMEM = pl.BlockSpec(memory_space=pltpu.VMEM)
SMEM = pl.BlockSpec(memory_space=pltpu.SMEM)


def dot(a, b, ca=1, cb=0):
    return lax.dot_general(
        a, b, (((ca,), (cb,)), ((), ())), precision=highest, preferred_element_type=jnp.float32
    )


def halves_of(value):
    high = value.astype(jnp.bfloat16)
    return high, (value - high.astype(jnp.float32)).astype(jnp.bfloat16)


def thirds_of(value):
    high = value.astype(jnp.bfloat16)
    rest = value - high.astype(jnp.float32)
    middle = rest.astype(jnp.bfloat16)
    return high, middle, (rest - middle.astype(jnp.float32)).astype(jnp.bfloat16)


def left_parts(value):
    high, middle, low = thirds_of(value)
    return jnp.concatenate([high, middle, high, middle, high, low], axis=1)


def right_parts(value):
    high, middle, low = thirds_of(value)
    return jnp.concatenate([high, high, middle, middle, low, high], axis=0)


def parts_dot(left, right):
    return lax.dot_general(
        left, right, (((1,), (0,)), ((), ())), preferred_element_type=jnp.float32
    )


def split_dot(a, b):
    a_high, a_low = halves_of(a)
    b_high, b_low = halves_of(b)
    part = lambda p, q: lax.dot_general(
        p, q, (((1,), (1,)), ((), ())), preferred_element_type=jnp.float32
    )
    return part(a_high, b_high) + (part(a_high, b_low) + part(a_low, b_high))


def inverse_factor_rows(groups):
    count = len(groups)
    full = (8, LANES)
    lane = lax.broadcasted_iota(jnp.int32, full, 1)
    sublane = lax.broadcasted_iota(jnp.int32, full, 0)
    d = list(groups)
    out = [None] * count
    for g in range(count):
        base = 8 * g
        inside = (lane >= base) & (lane < base + 8)
        own = d[g]
        cols = [jnp.broadcast_to(own[:, base + q : base + q + 1], full) for q in range(8)]
        e = [[None] * 8 for _ in range(8)]
        for q in range(8):
            for i in range(q, 8):
                e[i][q] = jnp.broadcast_to(cols[q][i : i + 1, :], full)
        y = []
        for i in range(8):
            row = jnp.broadcast_to(own[i : i + 1, :], full)
            y.append(jnp.where(inside, jnp.where(lane == base + i, 1.0, 0.0), row))
        scale = [lax.rsqrt(e[i][i]) for i in range(8)]
        for i in range(8):
            for j in range(i + 1):
                e[i][j] = e[i][j] * scale[i] * scale[j]
            y[i] = y[i] * scale[i]
        inv = [None] * 8
        low = [[None] * 8 for _ in range(8)]
        for p in range(0, 8, 2):
            q = p + 1
            inv[p] = 1.0 / e[p][p]
            inv[q] = e[p][p] / (e[p][p] * e[q][q] - e[q][p] * e[q][p])
            for i in range(q, 8):
                low[i][p] = e[i][p] * inv[p]
                e[i][q] = e[i][q] - low[i][p] * e[q][p]
            y[q] = y[q] - low[q][p] * y[p]
            for i in range(q + 1, 8):
                low[i][q] = e[i][q] * inv[q]
                for j in range(q + 1, i + 1):
                    e[i][j] = e[i][j] - low[i][p] * e[j][p] - low[i][q] * e[j][q]
                y[i] = y[i] - low[i][p] * y[p] - low[i][q] * y[q]
        rows = y[0] * lax.rsqrt(e[0][0])
        for i in range(1, 8):
            rows = jnp.where(sublane == i, y[i] * lax.rsqrt(e[i][i]), rows)
        out[g] = jnp.where(lane <= sublane + base, rows, 0.0)
        if g == count - 1:
            break
        s = [y[i] * inv[i] for i in range(8)]
        for i in range(6, -1, -1):
            for p in range(i + 1, 8):
                s[i] = s[i] - low[p][i] * s[p]
        s = [s[i] * scale[i] for i in range(8)]
        for r in range(g + 1, count):
            acc = jnp.where(inside, 0.0, d[r])
            for q in range(8):
                acc = acc - jnp.broadcast_to(d[r][:, base + q : base + q + 1], full) * s[q]
            d[r] = acc
    return out


def eliminate(x_ref, s_ref, block_ref, parts_ref, first, last):
    n = x_ref.shape[0]
    steps = n // LANES
    square = (LANES, LANES)
    eye = (
        lax.broadcasted_iota(jnp.int32, square, 0) == lax.broadcasted_iota(jnp.int32, square, 1)
    ).astype(jnp.float32)

    def step(k, carry):
        k0 = pl.multiple_of(k * LANES, LANES)
        here = pl.ds(k0, LANES)
        groups = [x_ref[pl.ds(k0 + 8 * r, 8), here] for r in range(LANES // 8)]
        for r, rows in enumerate(inverse_factor_rows(groups)):
            block_ref[8 * r : 8 * r + 8, :] = rows
        x_ref[here, here] = eye
        block = block_ref[...]
        parts_ref[...] = right_parts(x_ref[here, :])
        scaled = parts_dot(left_parts(block), parts_ref[...])
        parts_ref[...] = right_parts(scaled)
        solved = parts_dot(left_parts(block.T), parts_ref[...])
        x_ref[here, :] = scaled
        s_ref[here, :] = solved
        parts_ref[...] = right_parts(solved)

        def update(r, inner):
            there = pl.ds(pl.multiple_of(r * LANES, LANES), LANES)
            below = x_ref[there, here]
            x_ref[there, here] = jnp.zeros(square, jnp.float32)
            x_ref[there, :] = x_ref[there, :] - parts_dot(left_parts(below), parts_ref[...])
            return inner

        lax.fori_loop(k + 1, steps, update, 0)
        return carry

    lax.fori_loop(first, last, step, 0)


def open_kernel(last, at_ref, own_ref, other_ref, x_ref, s_ref, block_ref, parts_ref):
    core = at_ref[2]
    pieces, rows, _ = own_ref.shape
    for i in range(pieces):
        start = i * 2 * rows
        x_ref[pl.ds(pl.multiple_of(start + core * rows, rows), rows), :] = own_ref[i]
        x_ref[pl.ds(pl.multiple_of(start + (1 - core) * rows, rows), rows), :] = other_ref[i]
    eliminate(x_ref, s_ref, block_ref, parts_ref, 0, last)


def close_kernel(first, x_in, s_in, x_ref, s_ref, block_ref, parts_ref):
    del x_in, s_in
    eliminate(x_ref, s_ref, block_ref, parts_ref, first, x_ref.shape[0] // LANES)


def elimination(at, own, other, n, split):
    shape = jax.ShapeDtypeStruct((n, n), jnp.float32)
    common = dict(
        out_shape=(shape, shape),
        out_specs=(VMEM, VMEM),
        scratch_shapes=[
            pltpu.VMEM((LANES, LANES), jnp.float32),
            pltpu.VMEM((6 * LANES, n), jnp.bfloat16),
        ],
        compiler_params=pltpu.CompilerParams(vmem_limit_bytes=10 * 2**20),
    )
    cost = lambda share: pl.CostEstimate(
        flops=int(share * 40e9), bytes_accessed=8 * n * n, transcendentals=0
    )
    state = pl.pallas_call(
        functools.partial(open_kernel, split), in_specs=[SMEM, VMEM, VMEM], cost_estimate=cost(0.66), name="open_factor", **common
    )(at, own, other)
    return lambda x, s: pl.pallas_call(
        functools.partial(close_kernel, split),
        in_specs=[VMEM, VMEM],
        input_output_aliases={0: 0, 1: 1},
        cost_estimate=cost(0.34),
        name="close_factor",
        **common,
    )(x, s)[1], state


def contrib_kernel(pieces, at_ref, s_ref, own_ref, *refs):
    core, x, zh = at_ref[2], at_ref[3], at_ref[4]
    keep_ref, sent_ref, out_ref, w_ref = refs[len(pieces) :]
    depth = s_ref.shape[0]
    rows = own_ref.shape[0]
    w_ref[...] = own_ref[...]

    def step(k, carry):
        here = pl.ds(pl.multiple_of(k * LANES, LANES), LANES)
        pivot = w_ref[:, here]
        w_ref[:, here] = jnp.zeros((rows, LANES), jnp.float32)
        w_ref[...] = w_ref[...] - parts_dot(left_parts(pivot), right_parts(s_ref[here, :]))
        return carry

    lax.fori_loop(0, depth // LANES, step, 0)
    for ref, (dx, first, pairs) in zip(refs, pieces):

        def pair(m, carry, ref=ref, dx=dx, first=first):
            block = ref[pl.ds(2 * m, 2)].reshape(2 * TILE, depth)
            product = dot(w_ref[...], block, 1, 1)
            where = first + m
            for t, dz in enumerate((where, 3 * where - 1)):
                j = ((x + dx) & 3) * 4 + ((zh + dz) & 3)
                mine = (j // 8) == core
                inner = j % 8
                u = jnp.where(mine, keep_ref[inner], sent_ref[inner])
                out_ref[j, 0:rows, :] = u + product[:, t * TILE : (t + 1) * TILE]
            return carry

        lax.fori_loop(0, pairs, pair, 0)
    for k in range(16):
        for a in range(2):
            out_ref[k, rows + 8 * a : rows + 8 * a + 8, :] = out_ref[
                0, a * TILE + 8 * k : a * TILE + 8 * k + 8, :
            ]


PIECES = ((0, 0, 2), (-1, 0, 2), (1, 0, 2), (2, 0, 1), (2, 1, 1))


def contributions(at, solved, border, pieces, keep, sent):
    rows = border.shape[0]
    return pl.pallas_call(
        functools.partial(contrib_kernel, PIECES),
        out_shape=jax.ShapeDtypeStruct((16, rows + 16, TILE), jnp.float32),
        in_specs=[SMEM] + [VMEM] * (4 + len(pieces)),
        out_specs=VMEM,
        scratch_shapes=[pltpu.VMEM(border.shape, jnp.float32)],
        compiler_params=pltpu.CompilerParams(vmem_limit_bytes=10 * 2**20),
        name="contributions",
    )(at, solved, border, *pieces, keep, sent)


def split_kernel(at_ref, u_ref, keep_ref, send_ref):
    core = at_ref[2]
    for m in range(keep_ref.shape[0]):
        keep_ref[m] = u_ref[:, pl.ds(pl.multiple_of((2 * m + core) * TILE, TILE), TILE)]
        send_ref[m] = u_ref[:, pl.ds(pl.multiple_of((2 * m + 1 - core) * TILE, TILE), TILE)]


def split_update(at, update):
    rows, cols = update.shape
    shape = jax.ShapeDtypeStruct((cols // (2 * TILE), rows, TILE), jnp.float32)
    return pl.pallas_call(
        split_kernel,
        out_shape=(shape, shape),
        in_specs=[SMEM, VMEM],
        out_specs=(VMEM, VMEM),
        name="split_update",
    )(at, update)


def rows_dot(out_ref, rows_ref, x_ref):
    step = 256

    def chunk(m, carry):
        here = pl.ds(pl.multiple_of(m * step, step), step)
        out_ref[here, :] = dot(rows_ref[here, :], x_ref[...], 1, 1)
        return carry

    lax.fori_loop(0, out_ref.shape[0] // step, chunk, 0)


def panel_kernel(both_ref, panel_ref, x_ref, s_ref, block_ref, parts_ref, rows_ref):
    near = rows_ref.shape[0] // TILE
    for k in range(both_ref.shape[0]):
        for a in range(both_ref.shape[1] // 8):
            to, at = (rows_ref, a) if a < near else (x_ref, a - near)
            to[at * TILE + 8 * k : at * TILE + 8 * k + 8, :] = both_ref[k, 8 * a : 8 * a + 8, :]
    n = x_ref.shape[0]
    eliminate(x_ref, s_ref, block_ref, parts_ref, 0, n // LANES)
    row = lax.broadcasted_iota(jnp.int32, (n, n), 0)
    column = lax.broadcasted_iota(jnp.int32, (n, n), 1)
    x_ref[...] = jnp.where(column <= row, x_ref[...], 0.0)
    rows_dot(panel_ref, rows_ref, x_ref)


def panel(both):
    pieces, height, n = both.shape
    rows = pieces * height - n
    return pl.pallas_call(
        panel_kernel,
        out_shape=(jax.ShapeDtypeStruct((rows, n), jnp.float32), jax.ShapeDtypeStruct((n, n), jnp.float32)),
        in_specs=[VMEM],
        out_specs=(VMEM, VMEM),
        scratch_shapes=[
            pltpu.VMEM((n, n), jnp.float32),
            pltpu.VMEM((LANES, LANES), jnp.float32),
            pltpu.VMEM((6 * LANES, n), jnp.bfloat16),
            pltpu.VMEM((rows, n), jnp.float32),
        ],
        cost_estimate=pl.CostEstimate(flops=int(8e9), bytes_accessed=3 * 2**20, transcendentals=0),
        compiler_params=pltpu.CompilerParams(vmem_limit_bytes=10 * 2**20),
        name="panel",
    )(both)


def schur_kernel(at_ref, parent_ref, panel_ref, x_ref, *refs):
    far_refs = refs[:4]
    out_ref, rows_ref, solved_ref = refs[4:]
    x, zh = at_ref[3], at_ref[4]
    r = pl.program_id(0)

    @pl.when(r == 0)
    def _():
        for dx, far_ref in enumerate(far_refs):
            for dz in range(4):
                k = (x ^ dx) * 4 + (zh ^ dz)
                for a in range(far_ref.shape[1] // 8):
                    rows_ref[pl.ds(pl.multiple_of(a * TILE + 8 * k, 8), 8), :] = far_ref[
                        dz, 8 * a : 8 * a + 8, :
                    ]
        rows_dot(solved_ref, rows_ref, x_ref)

    step = out_ref.shape[0]
    here = pl.ds(pl.multiple_of(r * step, step), step)
    out_ref[...] = parent_ref[here, :] - split_dot(panel_ref[here, :], solved_ref[...])


def schur(at, parent, panel_rows, inverse, far):
    rows, cols = parent.shape
    n = panel_rows.shape[1]
    step = 256
    return pl.pallas_call(
        schur_kernel,
        grid=(rows // step,),
        out_shape=jax.ShapeDtypeStruct(parent.shape, jnp.float32),
        in_specs=[SMEM] + [VMEM] * 7,
        out_specs=pl.BlockSpec((step, cols), lambda r: (r, 0)),
        scratch_shapes=[pltpu.VMEM((rows, n), jnp.float32), pltpu.VMEM((rows, n), jnp.float32)],
        compiler_params=pltpu.CompilerParams(vmem_limit_bytes=16 * 2**20),
        name="schur",
    )(at, parent, panel_rows, inverse, *far)


def near_kernel(map_ref, at_ref, got_ref, base_ref, out_ref):
    i = at_ref[0]
    offset = got_ref.shape[1] - 16
    out_ref[...] = base_ref[...]

    def child(s, carry):
        for c in range(2):
            cb = map_ref[s, c]
            for a in range(2):
                ra = map_ref[s, 2 * i + a]

                @pl.when((ra >= 0) & (cb >= 0) & (cb < PANEL // TILE))
                def _():
                    rows = pl.ds(pl.multiple_of((ra - 8 * i) * 8, 8), 8)
                    lanes = pl.ds(pl.multiple_of(cb * TILE, TILE), TILE)
                    piece = got_ref[2 * s + c, offset + 8 * a : offset + 8 * a + 8, :]
                    out_ref[rows, lanes] = out_ref[rows, lanes] + piece

        return carry

    lax.fori_loop(0, map_ref.shape[0], child, 0)


def assemble_kernel(map_ref, at_ref, got_ref, parent_ref, out_ref):
    i = at_ref[0]
    g = at_ref[1]
    out_ref[...] = parent_ref[...]

    def child(s, carry):
        for c in range(2):
            cb = map_ref[s, 2 * g + c]
            for a in range(2):
                ra = map_ref[s, 2 * i + a]

                @pl.when((ra >= 0) & (cb >= 0))
                def _():
                    rows = pl.ds(pl.multiple_of((ra - 8 * i) * TILE, TILE), TILE)
                    lanes = pl.ds(pl.multiple_of((cb - 8 * g) * TILE, TILE), TILE)
                    piece = got_ref[2 * s + c, TILE * a : TILE * a + TILE, :]
                    out_ref[rows, lanes] = out_ref[rows, lanes] + piece

        return carry

    lax.fori_loop(0, map_ref.shape[0], child, 0)


def placed_sum(kernel, tile_map, at, got, base):
    return pl.pallas_call(
        kernel,
        out_shape=jax.ShapeDtypeStruct(base.shape, jnp.float32),
        in_specs=[SMEM, SMEM, VMEM, VMEM],
        out_specs=VMEM,
        compiler_params=pltpu.CompilerParams(vmem_limit_bytes=10 * 2**20),
    )(tile_map, at, got, base)


def gathered(value, axis):
    peers = lax.axis_size(axis)
    copies = jnp.broadcast_to(value[None], (peers, *value.shape))
    return lax.all_to_all(copies, axis, 0, 0, tiled=True)


def transposed_pairs():
    pairs = []
    for r in range(16):
        for k in range(16):

            def flat(row, group):
                x, zh = divmod(row, 4)
                y, rest = divmod(group, 4)
                zl, core = divmod(rest, 2)
                return (((y * 2 + zl) * 4 + x) * 4 + zh) * 2 + core

            pairs.append((flat(r, k), flat(k, r)))
    return pairs


def shifted(value, axis, by):
    peers = lax.axis_size(axis)
    return lax.ppermute(value, axis, [(i, (i + by) % peers) for i in range(peers)])


def flipped(value, axis):
    return [value] + [
        lax.ppermute(value, axis, [(i, i ^ by) for i in range(4)]) for by in (1, 2, 3)
    ]


def rows_to_slices(rows, count):
    total, cols = rows.shape
    tiles = total // (8 * count)
    return rows.reshape(tiles, count, 8, cols).transpose(1, 0, 2, 3).reshape(count, tiles * 8, cols)


def on_device(child_pivot, child_border, child_update, parent_front, tile_map):
    core = lax.axis_index("core")
    row = lax.axis_index(ROW)
    group = lax.axis_index(GRP)
    at = jnp.stack([row, group, core, lax.axis_index("x"), lax.axis_index("zh")]).astype(jnp.int32)
    border = child_border[0]
    n = child_pivot.shape[-1]

    part = lax.dynamic_slice_in_dim(child_pivot[0], core * 32, 32, 0)
    pivot = gathered(part, "zh")
    half = lax.dynamic_slice_in_dim(border, core * TILE, TILE, 0)
    corner = rows_to_slices(parent_front[:, :PANEL], 16).reshape(4, 2, 2, 64, PANEL)
    quarters = [lax.ppermute(corner[q], GRP, [(0, 4 * q)]) for q in (1, 2, 3)]
    corner = jnp.where(lax.axis_index("y") == 0, corner[0], quarters[0] + quarters[1] + quarters[2])
    pivot, half, update, corner = lax.optimization_barrier((pivot, half, child_update[0], corner))
    up = shifted(half, "zh", 1)
    down = shifted(half, "zh", -1)
    far0 = shifted(up[: TILE // 2], "zh", 1)
    far1 = shifted(down[TILE // 2 :], "zh", -1)
    column = jnp.stack([half, up, down, jnp.concatenate([far0, far1], axis=0)])
    pivot = gathered(pivot, "x")
    keep, send = split_update(at, update)
    sent = lax.ppermute(send, "core", [(0, 1), (1, 0)])
    eighth = lax.ppermute(corner[1], GRP, [(4 * y, 4 * y + 2) for y in range(4)])
    corner = jnp.where(lax.axis_index("zl") == 0, corner[0], eighth)
    pivot, corner, keep, sent, column = lax.optimization_barrier((pivot, corner, keep, sent, column))
    pivot = pivot.reshape(16, 32, n)
    other = lax.ppermute(pivot, "core", [(0, 1), (1, 0)])
    last = lax.ppermute(corner[1], GRP, [(2 * m, 2 * m + 1) for m in range(8)])
    base = jnp.where(core == 0, corner[0], last)

    split = 5
    close, state = elimination(at, pivot, other, n, split)
    up = shifted(column, "x", 1)
    down = shifted(column, "x", -1)
    x_state, s_state, up, down = lax.optimization_barrier((*state, up, down))
    far0 = shifted(up[:2], "x", 1)
    far1 = shifted(down[2:], "x", -1)
    solved = close(x_state, s_state)
    send = contributions(at, solved, border, (column, up, down, far0, far1), keep, sent)
    got = lax.all_to_all(send, GRP, 0, 0, tiled=True)

    mine = placed_sum(near_kernel, tile_map, at, got, base)
    far = lax.ppermute(mine, AXES, transposed_pairs())
    top = gathered(mine[:16], "x")[0]
    far, top = lax.optimization_barrier((far, top))
    far = flipped(far, "zh")
    top = gathered(top, "zh")[0]
    *far, top = lax.optimization_barrier((*far, top))
    far = flipped(jnp.stack(far), "x")
    both = gathered(jnp.concatenate([mine, top], axis=0), GRP)
    parent = placed_sum(assemble_kernel, tile_map, at, got, parent_front)
    both, parent = lax.optimization_barrier((both, parent))
    panel_rows, inverse = panel(both)
    schur_block = schur(at, parent, panel_rows, inverse, far)
    return (schur_block, panel_rows)


def solution(mesh):
    fine = Mesh(mesh.devices.reshape(SIZES), AXES)
    placed = (
        P(SUB, ROW, None),
        P(SUB, ROW, None),
        P(SUB, ROW, "core"),
        P(ROW, GRP),
        P(),
    )
    return jax.shard_map(
        on_device,
        mesh=fine,
        in_specs=placed,
        out_specs=(P(ROW, GRP), P(ROW, None)),
        check_vma=False,
    )
```
